32 devices in a mesh: seq: 4 (over y, x), fsdp: 8 (over z, core).
Axes of the slice: x: 2, y: 2, z: 4, core: 2. Of those that a mesh axis runs over, the one named last changes fastest.
Arguments:
- tokens: bfloat16 [16, 1024, 2048], P('fsdp', 'seq'), may hold values from -6 to 6
- cotangent: bfloat16 [16, 1024, 2048], P('fsdp', 'seq'), may hold values from -6 to 6
- lengths: int32 [16], P('fsdp'), may hold values from 512 to 1024, as said below
- decay: float32 [16, 1024], P('seq'), may hold values from -1 to 0
- query_weight: bfloat16 [2048, 2048], P('fsdp'), may hold values from -0.125 to 0.125
- key_weight: bfloat16 [2048, 2048], P('fsdp'), may hold values from -0.125 to 0.125
- value_weight: bfloat16 [2048, 2048], P('fsdp'), may hold values from -0.125 to 0.125
- outgate_weight: bfloat16 [2048, 2048], P('fsdp'), may hold values from -0.125 to 0.125
- output_weight: bfloat16 [2048, 2048], P('fsdp'), may hold values from -0.125 to 0.125
- left_weight: bfloat16 [5632, 2048], P('fsdp'), may hold values from -0.125 to 0.125
- right_weight: bfloat16 [5632, 2048], P('fsdp'), may hold values from -0.125 to 0.125
- down_weight: bfloat16 [5632, 2048], P('fsdp'), may hold values from -0.078125 to 0.078125
Outputs:
- layer_out: bfloat16 [16, 1024, 2048], P('fsdp', 'seq')
- input_grad: bfloat16 [16, 1024, 2048], P('fsdp', 'seq')
- query_grad: float32 [2048, 2048], P('fsdp')
- key_grad: float32 [2048, 2048], P('fsdp')
- value_grad: float32 [2048, 2048], P('fsdp')
- outgate_grad: float32 [2048, 2048], P('fsdp')
- output_grad: float32 [2048, 2048], P('fsdp')
- left_grad: float32 [5632, 2048], P('fsdp')
- right_grad: float32 [5632, 2048], P('fsdp')
- down_grad: float32 [5632, 2048], P('fsdp')
The draws below stay inside these ranges and needn't reach their ends.
Inputs may be any that keep to these rules, and one draw needn't show every extreme that they name: `lengths`: some sequence has all 1024 slots valid and another exactly 512.
All inputs are finite; a program needn't handle non-finite values.
Results may differ from the reference program's by a relative error of at most 0.02.
Values may be sent and summed in bfloat16 or wider, within the bound.
No kernel may reach another device: no remote copies, remote signals or barrier semaphores. Data moves between devices by JAX's collectives and lax.ppermute only.
A program may use at most 576 MiB of HBM per device.

```python
import math
import jax
import jax.numpy as jnp
from jax import lax

D = 2048
MIXER_CHANNELS = 16
HEAD_DIM = 128
FF = 5632
BLOCK = 256
CONTEXT_LENGTH = 1024
SEQS = 16


def draw_lengths(key, part):
    matched_vector_collection = jax.random.split(jax.random.fold_in(key, 11), 2)
    values = jax.random.randint(matched_vector_collection[0], (SEQS,), CONTEXT_LENGTH // 2, CONTEXT_LENGTH + 1)
    element_permutation = jax.random.permutation(matched_vector_collection[1], SEQS)
    values = values.at[element_permutation[0]].set(CONTEXT_LENGTH)
    values = values.at[element_permutation[1]].set(CONTEXT_LENGTH // 2)
    return values.astype(jnp.int32)


def draw_decay(key, part):
    matched_vector_collection = jax.random.split(jax.random.fold_in(key, 23), 7)
    fast_share = 0.5
    fast_heads = jax.random.uniform(matched_vector_collection[0], (MIXER_CHANNELS, 1)) < fast_share
    fast_rate = jnp.exp(jax.random.uniform(matched_vector_collection[1], (MIXER_CHANNELS, 1), minval=math.log(0.02), maxval=math.log(0.033)))
    slow_rate = jnp.exp(jax.random.uniform(matched_vector_collection[2], (MIXER_CHANNELS, 1), minval=math.log(0.08), maxval=math.log(0.4))) / CONTEXT_LENGTH
    default_forgetting_factor = jnp.where(fast_heads, fast_rate, slow_rate)
    context_portion = jnp.exp(jax.random.uniform(matched_vector_collection[3], (MIXER_CHANNELS, 8, 1), minval=-0.5, maxval=0.5))
    context_portion = jnp.broadcast_to(context_portion, (MIXER_CHANNELS, 8, CONTEXT_LENGTH // 8)).reshape(MIXER_CHANNELS, CONTEXT_LENGTH)
    rough_approximation = jnp.exp(jax.random.uniform(matched_vector_collection[4], (MIXER_CHANNELS, CONTEXT_LENGTH), minval=-0.5, maxval=0.5))
    element_permutation = jax.random.permutation(matched_vector_collection[5], CONTEXT_LENGTH)[:3]
    group_position_total = jnp.zeros((CONTEXT_LENGTH,), jnp.float32).at[element_permutation].set(1.0)
    element_cluster = jax.random.uniform(matched_vector_collection[6], (MIXER_CHANNELS, CONTEXT_LENGTH), minval=0.223, maxval=0.511) * group_position_total[None, :]
    return (-(default_forgetting_factor * context_portion * rough_approximation + element_cluster)).astype(jnp.float32)


def level_of(key, extent, cuts, least, largest):
    def one(position, shards_of):
        heights = jax.random.uniform(jax.random.fold_in(jax.random.fold_in(key, 6), position), (shards_of,), jnp.float32, least / len(cuts), largest / len(cuts))
        return jnp.repeat(jnp.exp(heights), extent[position] // shards_of).reshape((-1,) + (1,) * (len(extent) - position - 1))

    gain = one(*cuts[0])
    for cut in cuts[1:]:
        gain = gain * one(*cut)
    return gain


def normal_values(stream_key, extent, deviation, limit, shards=(), kind=jnp.bfloat16):
    level = level_of(stream_key, extent, shards, -0.22, 0.18) if shards else 1.0
    entries = jax.random.normal(stream_key, extent, jnp.float32) * deviation * level
    return jnp.minimum(jnp.maximum(entries, -limit), limit).astype(kind)


def setup_inputs(seed: int = 0) -> dict:
    splits = jax.random.split(jax.random.key(seed), 13)
    tokens = normal_values(splits[0], (SEQS, CONTEXT_LENGTH, D), 1.0, 6.0, ((0, 8), (1, 4)))
    cotangent = normal_values(splits[1], (SEQS, CONTEXT_LENGTH, D), 1.0, 6.0, ((0, 8), (1, 4)))
    lengths = draw_lengths(jax.random.fold_in(splits[12], 71), 0)
    decay = draw_decay(jax.random.fold_in(splits[12], 71), 0)
    query_weight = normal_values(splits[4], (D, D), D ** -0.5, 0.125, ((0, 8),))
    key_weight = normal_values(splits[5], (D, D), D ** -0.5, 0.125, ((0, 8),))
    value_weight = normal_values(splits[6], (D, D), D ** -0.5, 0.125, ((0, 8),))
    outgate_weight = normal_values(splits[7], (D, D), D ** -0.5, 0.125, ((0, 8),))
    output_weight = normal_values(splits[8], (D, D), D ** -0.5, 0.125, ((0, 8),))
    left_weight = normal_values(splits[9], (FF, D), D ** -0.5, 0.125, ((0, 8),))
    right_weight = normal_values(splits[10], (FF, D), D ** -0.5, 0.125, ((0, 8),))
    down_weight = normal_values(splits[11], (FF, D), FF ** -0.5, 0.078125, ((0, 8),))
    return {"tokens": tokens, "cotangent": cotangent, "lengths": lengths, "decay": decay, "query_weight": query_weight, "key_weight": key_weight, "value_weight": value_weight, "outgate_weight": outgate_weight, "output_weight": output_weight, "left_weight": left_weight, "right_weight": right_weight, "down_weight": down_weight}


highest = lax.Precision.HIGHEST
eps_norm = 1e-06

@jax.custom_vjp
def low(v):
    return lax.optimization_barrier(v.astype(jnp.bfloat16)).astype(jnp.float32)

@jax.custom_vjp
def low_back(v):
    return v

def low_keep(v):
    return (low(v), None)

def low_pass(kept, grad):
    return (grad,)

def back_keep(v):
    return (v, None)

def back_low(kept, grad):
    return (low(grad),)
low.defvjp(low_keep, low_pass)
low_back.defvjp(back_keep, back_low)

def scaled(values):
    return values * lax.rsqrt(lax.optimization_barrier(jnp.mean(values * values, axis=-1, keepdims=True)) + eps_norm)

def block_step(state_now, inputs):
    query_block, key_block, value_block, decay_sums = inputs
    size_block = decay_sums.shape[-1]
    row_ids = lax.broadcasted_iota(jnp.int32, (size_block, size_block), 0)
    col_ids = lax.broadcasted_iota(jnp.int32, (size_block, size_block), 1)
    causal = (row_ids >= col_ids)[None]
    spread = decay_sums[:, :, None] - decay_sums[:, None, :]
    weights = jnp.where(causal, jnp.exp(jnp.where(causal, spread, 0.0)), 0.0)
    scores = jnp.einsum('thi,shi->hts', query_block, key_block, precision=highest) * weights
    inner_part = jnp.einsum('hts,shj->thj', scores, value_block, precision=highest)
    carried = jnp.einsum('thi,hij->thj', query_block, state_now, precision=highest) * jnp.exp(decay_sums).T[:, :, None]
    tail_decay = jnp.exp(decay_sums[:, -1:] - decay_sums).T
    state_next = jnp.exp(decay_sums[:, -1])[:, None, None] * state_now + jnp.einsum('shi,shj->hij', key_block * tail_decay[:, :, None], value_block, precision=highest)
    return (state_next, inner_part + carried)

def lightning(queries, key_rows, values, log_decay):
    slot_count, head_count, head_width = queries.shape
    block_count = slot_count // BLOCK
    decay_sums = jnp.cumsum(log_decay.reshape(head_count, block_count, BLOCK), axis=-1).transpose(1, 0, 2)
    shape_blocks = (block_count, BLOCK, head_count, head_width)
    start_state = jnp.zeros((head_count, head_width, head_width), jnp.float32)
    _, outputs = lax.scan(jax.checkpoint(block_step), start_state, (queries.reshape(shape_blocks), key_rows.reshape(shape_blocks), values.reshape(shape_blocks), decay_sums))
    return outputs.reshape(slot_count, head_count, head_width)

def layer_forward(tokens_wide, valid_rows, decay, query_weight, key_weight, value_weight, outgate_weight, output_weight, left_weight, right_weight, down_weight):
    seq_count, slot_count, feat_width = tokens_wide.shape
    normed = low(scaled(tokens_wide))

    def project(weight):
        return jnp.einsum('gtd,ed->gte', normed, weight, precision=highest)
    pre_query = low_back(low(project(query_weight)))
    pre_key = low_back(low(project(key_weight)))
    pre_value = low_back(low(project(value_weight)))
    outgate = low_back(project(outgate_weight))
    heads_shape = (seq_count, slot_count, MIXER_CHANNELS, HEAD_DIM)
    attn_rows = jax.vmap(lightning, in_axes=(0, 0, 0, None))(jax.nn.silu(pre_query).reshape(heads_shape), jax.nn.silu(pre_key).reshape(heads_shape), pre_value.reshape(heads_shape), decay)
    attn_rows = low_back(low(attn_rows.reshape(seq_count, slot_count, feat_width)))
    gated_rows = low(scaled(attn_rows) * outgate)
    branch = low_back(jnp.einsum('gte,de->gtd', gated_rows, output_weight, precision=highest))
    residual = tokens_wide + branch
    resid_normed = low(scaled(residual))
    left_rows = low_back(jnp.einsum('gtd,fd->gtf', resid_normed, left_weight, precision=highest))
    right_rows = low_back(jnp.einsum('gtd,fd->gtf', resid_normed, right_weight, precision=highest))
    product = low(left_rows * right_rows)
    ffn_out = low_back(jnp.einsum('gtf,fd->gtd', product, down_weight, precision=highest))
    return valid_rows[:, :, None] * (residual + ffn_out)

def reference(tokens, cotangent, lengths, decay, query_weight, key_weight, value_weight, outgate_weight, output_weight, left_weight, right_weight, down_weight):
    seq_total, slot_count, feat_width = tokens.shape
    group_size = max(1, min(seq_total, 4096 // slot_count))
    while seq_total % group_size != 0:
        group_size = group_size - 1
    group_count = seq_total // group_size
    weights_wide = tuple((weight_arg.astype(jnp.float32) for weight_arg in (query_weight, key_weight, value_weight, outgate_weight, output_weight, left_weight, right_weight, down_weight)))
    positions = lax.broadcasted_iota(jnp.int32, (seq_total, slot_count), 1)
    valid_all = (positions < lengths[:, None].astype(jnp.int32)).astype(jnp.float32)
    group_shape = (group_count, group_size, slot_count, feat_width)

    def group_step(totals, inputs):
        tokens_group, cot_group, valid_group = inputs

        def forward_fn(tokens_wide, *weight_list):
            return layer_forward(tokens_wide, valid_group, decay, *weight_list)
        out_group, pullback = jax.vjp(forward_fn, tokens_group.astype(jnp.float32), *weights_wide)
        gradients = pullback(cot_group.astype(jnp.float32))
        new_totals = tuple((total_one + grad_one for total_one, grad_one in zip(totals, gradients[1:])))
        return (new_totals, (out_group.astype(jnp.bfloat16), gradients[0].astype(jnp.bfloat16)))
    start_totals = tuple((jnp.zeros(weight_arg.shape, jnp.float32) for weight_arg in weights_wide))
    totals, (outputs, input_grads) = lax.scan(group_step, start_totals, (tokens.reshape(group_shape), cotangent.reshape(group_shape), valid_all.reshape(group_count, group_size, slot_count)))
    layer_out = outputs.reshape(seq_total, slot_count, feat_width)
    input_grad = input_grads.reshape(seq_total, slot_count, feat_width)
    return (layer_out, input_grad, totals[0], totals[1], totals[2], totals[3], totals[4], totals[5], totals[6], totals[7])
```

```python
import functools

import jax
import jax.numpy as jnp
from jax import lax
from jax.experimental import pallas as pl
from jax.experimental.pallas import tpu as pltpu
from jax.sharding import PartitionSpec as P

HEAD = 128
EPS = 1e-06
F32 = jnp.float32
LOW = jnp.bfloat16


def swap_seq(x, bit):
    size = lax.axis_size("seq")
    return lax.ppermute(x, "seq", [(i, i ^ bit) for i in range(size)])


def swap_core(x):
    size = lax.axis_size("fsdp")
    return lax.ppermute(x, "fsdp", [(i, i ^ 1) for i in range(size)])


def spread(units):
    size = lax.axis_size("seq")
    if size != 4:
        return [units] + [[swap_seq(u, i) for u in units] for i in range(1, size)]
    by_x = [swap_seq(u, 1) for u in units]
    by_y = [swap_seq(u, 2) for u in units]
    half = (len(units) + 1) // 2
    both = [swap_seq(u, 2) for u in by_x[:half]] + [swap_seq(u, 1) for u in by_y[half:]]
    return [units, by_x, by_y, both]


def collect(parts):
    size = lax.axis_size("seq")
    wide = lambda x: x.astype(F32)
    count = len(parts[0])
    if size != 4:
        out = []
        for b in range(count):
            total = wide(parts[0][b])
            for i in range(1, size):
                total = total + wide(swap_seq(parts[i][b].astype(LOW), i))
            out.append(total)
        return out
    half = (count + 1) // 2
    out = []
    for b in range(count):
        first, second = (1, 2) if b < half else (2, 1)
        passed = swap_seq(parts[3][b].astype(LOW), first)
        direct = swap_seq(parts[first][b].astype(LOW), first)
        joined = swap_seq((wide(parts[second][b]) + wide(passed)).astype(LOW), second)
        out.append(wide(parts[0][b]) + wide(direct) + wide(joined))
    return out


def times_rows(left_side, weight):
    return lax.dot_general(
        left_side, weight, (((1,), (1,)), ((), ())), preferred_element_type=F32
    )


def times(left_side, weight):
    return lax.dot_general(
        left_side, weight, (((1,), (0,)), ((), ())), preferred_element_type=F32
    )


def rows_outer(left_side, right_side):
    return lax.dot_general(
        left_side, right_side, (((0,), (0,)), ((), ())), preferred_element_type=F32
    )


def norm_factor(values):
    return lax.rsqrt(jnp.mean(values * values, axis=-1, keepdims=True) + EPS)


def norm_back(values, factor, grad_in):
    inner_mean = jnp.mean(grad_in * values, axis=-1, keepdims=True)
    return factor * grad_in - values * (factor * factor * factor) * inner_mean


def sigmoid(x):
    return 1.0 / (1.0 + jnp.exp(-x))


def dot_nt(a, b):
    return lax.dot_general(a, b, (((1,), (1,)), ((), ())), preferred_element_type=F32)


def dot_nn(a, b):
    return lax.dot_general(a, b, (((1,), (0,)), ((), ())), preferred_element_type=F32)


def dot_tn(a, b):
    return lax.dot_general(a, b, (((0,), (0,)), ((), ())), preferred_element_type=F32)


def decay_weights(down, across):
    count = down.shape[0]
    rows = lax.broadcasted_iota(jnp.int32, (count, count), 0)
    cols = lax.broadcasted_iota(jnp.int32, (count, count), 1)
    apart = down[:, :1] - across
    return jnp.where(rows >= cols, jnp.exp(jnp.minimum(apart, 0.0)), 0.0)


def attend_kernel(s_ref, pre_ref, down_ref, across_ref, out_ref, attn_ref, square_ref, state_ref):
    me = s_ref[0]
    head = pl.program_id(1)
    blocks = pre_ref.shape[0]
    state_ref[...] = jnp.zeros_like(state_ref)

    def step(c, carry):
        i = lax.bitwise_xor(jnp.int32(c), me)
        pre_q = pre_ref[i, 0, :, 0:HEAD].astype(F32)
        pre_k = pre_ref[i, 0, :, HEAD : 2 * HEAD].astype(F32)
        value = pre_ref[i, 0, :, 2 * HEAD : 3 * HEAD]
        gate = pre_ref[i, 0, :, 3 * HEAD : 4 * HEAD].astype(F32)
        query = (pre_q * sigmoid(pre_q)).astype(LOW)
        key = pre_k * sigmoid(pre_k)
        down = down_ref[0, c]
        across = across_ref[0, pl.ds(c, 1), :]
        weights = decay_weights(down, across)
        scores = (dot_nt(query, key.astype(LOW)) * weights).astype(LOW)
        state = state_ref[...]
        out = dot_nn(scores, value) + dot_nn(query, state.astype(LOW)) * jnp.exp(down)
        last = down[down.shape[0] - 1 :, :]
        tail = (key * jnp.exp(last - down)).astype(LOW)
        state_ref[...] = jnp.exp(last) * state + dot_tn(tail, value)
        low = out.astype(LOW)
        attn_ref[i, 0] = low
        rounded = low.astype(F32)
        out_ref[i, 0] = (rounded * gate).astype(LOW)
        before = jnp.where(head == 0, 0.0, square_ref[i, 0])
        square_ref[i, 0] = before + rounded * rounded
        return carry

    lax.fori_loop(0, blocks, step, 0)


def attend_back_kernel(
    s_ref,
    pre_ref,
    attn_ref,
    grad_ref,
    factor_ref,
    inner_ref,
    down_ref,
    across_ref,
    out_ref,
    gated_ref,
    states_ref,
    state_ref,
):
    me = s_ref[0]
    blocks = pre_ref.shape[0]
    state_ref[...] = jnp.zeros_like(state_ref)

    def forward(c, carry):
        i = lax.bitwise_xor(jnp.int32(c), me)
        pre_k = pre_ref[i, 0, :, HEAD : 2 * HEAD].astype(F32)
        value = pre_ref[i, 0, :, 2 * HEAD : 3 * HEAD]
        key = pre_k * sigmoid(pre_k)
        down = down_ref[0, c]
        last = down[down.shape[0] - 1 :, :]
        tail = (key * jnp.exp(last - down)).astype(LOW)
        state = state_ref[...]
        states_ref[c] = state.astype(LOW)
        state_ref[...] = jnp.exp(last) * state + dot_tn(tail, value)
        return carry

    lax.fori_loop(0, blocks, forward, 0)
    state_ref[...] = jnp.zeros_like(state_ref)

    def backward(n, carry):
        c = blocks - 1 - n
        i = lax.bitwise_xor(jnp.int32(c), me)
        pre_q = pre_ref[i, 0, :, 0:HEAD].astype(F32)
        pre_k = pre_ref[i, 0, :, HEAD : 2 * HEAD].astype(F32)
        value = pre_ref[i, 0, :, 2 * HEAD : 3 * HEAD]
        gate = pre_ref[i, 0, :, 3 * HEAD : 4 * HEAD].astype(F32)
        attn = attn_ref[i, 0].astype(F32)
        grad = grad_ref[i, 0].astype(F32)
        factor = factor_ref[i, 0]
        scaled = attn * factor
        gated_ref[i, 0] = (scaled * gate).astype(LOW)
        grad_gate = grad * scaled
        grad_attn = (factor * (grad * gate) - attn * inner_ref[i, 0]).astype(LOW)
        sig_q = sigmoid(pre_q)
        sig_k = sigmoid(pre_k)
        query = pre_q * sig_q
        key = pre_k * sig_k
        query_low = query.astype(LOW)
        key_low = key.astype(LOW)
        down = down_ref[0, c]
        across = across_ref[0, pl.ds(c, 1), :]
        last = down[down.shape[0] - 1 :, :]
        weights = decay_weights(down, across)
        scores = (dot_nt(query_low, key_low) * weights).astype(LOW)
        paired = (dot_nt(grad_attn, value) * weights).astype(LOW)
        tail = jnp.exp(last - down)
        later = state_ref[...]
        later_low = later.astype(LOW)
        grown = jnp.exp(down)
        grad_q = dot_nn(paired, key_low) + grown * dot_nt(grad_attn, states_ref[c])
        grad_k = dot_tn(paired, query_low) + tail * dot_nt(value, later_low)
        grad_v = dot_tn(scores, grad_attn) + tail * dot_nn(key_low, later_low)
        state_ref[...] = jnp.exp(last) * later + dot_tn((query * grown).astype(LOW), grad_attn)
        out_ref[i, 0, :, 0:HEAD] = (grad_q * (sig_q * (1.0 + pre_q * (1.0 - sig_q)))).astype(LOW)
        out_ref[i, 0, :, HEAD : 2 * HEAD] = (
            grad_k * (sig_k * (1.0 + pre_k * (1.0 - sig_k)))
        ).astype(LOW)
        out_ref[i, 0, :, 2 * HEAD : 3 * HEAD] = grad_v.astype(LOW)
        out_ref[i, 0, :, 3 * HEAD : 4 * HEAD] = grad_gate.astype(LOW)
        return carry

    lax.fori_loop(0, blocks, backward, 0)


def attend(me, pre, down, across):
    blocks, seqs, slots, width = pre.shape
    heads = width // (4 * HEAD)
    one = pl.BlockSpec((blocks, 1, slots, HEAD), lambda b, h, s: (0, b, 0, h))
    return pl.pallas_call(
        attend_kernel,
        grid_spec=pltpu.PrefetchScalarGridSpec(
            num_scalar_prefetch=1,
            grid=(seqs, heads),
            in_specs=[
                pl.BlockSpec((blocks, 1, slots, 4 * HEAD), lambda b, h, s: (0, b, 0, h)),
                pl.BlockSpec((1, blocks, slots, HEAD), lambda b, h, s: (h, 0, 0, 0)),
                pl.BlockSpec((1, blocks, slots), lambda b, h, s: (h, 0, 0)),
            ],
            out_specs=[
                one,
                one,
                pl.BlockSpec((blocks, 1, slots, HEAD), lambda b, h, s: (0, b, 0, 0)),
            ],
            scratch_shapes=[pltpu.VMEM((HEAD, HEAD), F32)],
        ),
        out_shape=[
            jax.ShapeDtypeStruct((blocks, seqs, slots, heads * HEAD), LOW),
            jax.ShapeDtypeStruct((blocks, seqs, slots, heads * HEAD), LOW),
            jax.ShapeDtypeStruct((blocks, seqs, slots, HEAD), F32),
        ],
        compiler_params=pltpu.CompilerParams(
            dimension_semantics=("arbitrary", "arbitrary"), vmem_limit_bytes=32 << 20
        ),
        cost_estimate=pl.CostEstimate(
            flops=2_500_000_000, bytes_accessed=16 << 20, transcendentals=4_000_000
        ),
        name="attend",
    )(me, pre, down, across)


def attend_back(me, pre, attn, grad, factor, inner, down, across):
    blocks, seqs, slots, width = pre.shape
    heads = width // (4 * HEAD)
    one = pl.BlockSpec((blocks, 1, slots, HEAD), lambda b, h, s: (0, b, 0, h))
    four = pl.BlockSpec((blocks, 1, slots, 4 * HEAD), lambda b, h, s: (0, b, 0, h))
    same = pl.BlockSpec((blocks, 1, slots, HEAD), lambda b, h, s: (0, b, 0, 0))
    return pl.pallas_call(
        attend_back_kernel,
        grid_spec=pltpu.PrefetchScalarGridSpec(
            num_scalar_prefetch=1,
            grid=(seqs, heads),
            in_specs=[
                four,
                one,
                one,
                same,
                same,
                pl.BlockSpec((1, blocks, slots, HEAD), lambda b, h, s: (h, 0, 0, 0)),
                pl.BlockSpec((1, blocks, slots), lambda b, h, s: (h, 0, 0)),
            ],
            out_specs=[four, one],
            scratch_shapes=[
                pltpu.VMEM((blocks, HEAD, HEAD), LOW),
                pltpu.VMEM((HEAD, HEAD), F32),
            ],
        ),
        out_shape=[
            jax.ShapeDtypeStruct((blocks, seqs, slots, width), LOW),
            jax.ShapeDtypeStruct((blocks, seqs, slots, heads * HEAD), LOW),
        ],
        compiler_params=pltpu.CompilerParams(
            dimension_semantics=("arbitrary", "arbitrary"), vmem_limit_bytes=40 << 20
        ),
        cost_estimate=pl.CostEstimate(
            flops=8_000_000_000, bytes_accessed=32 << 20, transcendentals=8_000_000
        ),
        name="attend_back",
    )(me, pre, attn, grad, factor, inner, down, across)


def paired_heads(rows):
    return rows % HEAD == 0 and 2 * rows // HEAD == lax.axis_size("seq") == 4


def gather_projections(weights, me_seq, me_fsdp):
    rows, feat = weights[0].shape
    size = lax.axis_size("seq")
    if not paired_heads(rows):
        picked = []
        for weight in weights:
            full = lax.all_gather(weight, "fsdp", axis=0, tiled=True)
            full = full.reshape(-1, size, HEAD, feat)
            picked.append(lax.dynamic_index_in_dim(full, me_seq, 1, keepdims=False))
        return jnp.stack(picked, 1).reshape(-1, feat)
    core = me_fsdp % 2
    own = [
        lax.dynamic_slice_in_dim(weight, (me_seq % 2) * HEAD, HEAD, 0) for weight in weights
    ]
    first = jnp.concatenate(own[:2], 0)
    second = jnp.concatenate(own[2:], 0)
    keep = jnp.where(core == 0, first, second)
    give = jnp.where(core == 0, second, first)
    got = swap_core(give)
    return lax.all_gather(
        jnp.where(core == me_seq // 2, keep, got), "fsdp", axis=0, tiled=True
    )


def scatter_projections(grad, rows, me_seq, me_fsdp):
    feat = grad.shape[1]
    size = lax.axis_size("seq")
    if not paired_heads(rows):
        parts = grad.reshape(-1, 1, 4, HEAD, feat)
        result = []
        for which in range(4):
            full = jnp.zeros((parts.shape[0], size, HEAD, feat), grad.dtype)
            full = lax.dynamic_update_slice_in_dim(full, parts[:, :, which], me_seq, 1)
            part = lax.psum_scatter(
                full.reshape(-1, feat), "fsdp", scatter_dimension=0, tiled=True
            )
            result.append(lax.psum(part, "seq").astype(F32))
        return result
    core = me_fsdp % 2
    mine = lax.psum_scatter(grad, "fsdp", scatter_dimension=0, tiled=True)
    pieces = spread([mine[:HEAD], mine[HEAD:]])
    pieces = [jnp.concatenate(p, 0) for p in pieces]
    straight = (core ^ (me_seq // 2)) == 0
    keep = [jnp.where(straight, pieces[j], pieces[2 + j]) for j in range(2)]
    give = [jnp.where(straight, pieces[2 + j], pieces[j]) for j in range(2)]
    got = [swap_core(g) for g in give]
    even = me_seq % 2 == 0
    keep = [jnp.where(even, keep[0], keep[1]), jnp.where(even, keep[1], keep[0])]
    got = [jnp.where(even, got[0], got[1]), jnp.where(even, got[1], got[0])]
    first = [jnp.where(core == 0, k, g) for k, g in zip(keep, got)]
    second = [jnp.where(core == 0, g, k) for k, g in zip(keep, got)]
    result = []
    for pair in (first, second):
        for part in range(2):
            span = slice(part * HEAD, (part + 1) * HEAD)
            result.append(jnp.concatenate([p[span] for p in pair], 0).astype(F32))
    return result


def in_order(pieces, me_seq):
    size = len(pieces)
    stack = jnp.stack(pieces)
    bit = 1
    index = lax.iota(jnp.int32, size)
    while bit < size:
        turned = jnp.stack([stack[i ^ bit] for i in range(size)])
        stack = jnp.where((me_seq & bit) != 0, turned, stack)
        bit *= 2
    return [stack[i] for i in range(size)]


def place_rows(units_by_piece, me_seq):
    rows = sum(u.shape[0] for u in units_by_piece[0])
    feat = units_by_piece[0][0].shape[1]
    out = jnp.zeros((rows * len(units_by_piece), feat), F32)
    for i, units in enumerate(units_by_piece):
        start = (me_seq ^ i) * rows
        for unit in units:
            out = lax.dynamic_update_slice_in_dim(out, unit.astype(F32), start, 0)
            start = start + unit.shape[0]
    return out


def halves(x):
    cut = max(16, x.shape[0] // 32 * 16)
    return [x[:cut], x[cut:]]


def on_device(
    tokens,
    cotangent,
    lengths,
    decay,
    query_weight,
    key_weight,
    value_weight,
    outgate_weight,
    output_weight,
    left_weight,
    right_weight,
    down_weight,
):
    seqs, slots, feat = tokens.shape
    size = lax.axis_size("seq")
    me_seq = lax.axis_index("seq")
    me_fsdp = lax.axis_index("fsdp")
    rows_all = size * seqs * slots
    span = range(seqs)

    def whole(pieces):
        return jnp.concatenate([u for units in pieces for u in units], 0)

    def cut(rows):
        return [rows[b * slots : (b + 1) * slots] for b in span]

    wide = [tokens[b].astype(F32) for b in span]
    factor_in = [norm_factor(w) for w in wide]
    normed = [(w * r).astype(LOW) for w, r in zip(wide, factor_in)]

    project = gather_projections(
        (query_weight, key_weight, value_weight, outgate_weight), me_seq, me_fsdp
    )
    out_rows = output_weight.shape[0]
    out_own = lax.dynamic_index_in_dim(
        output_weight.reshape(out_rows, -1, size, HEAD), me_seq, 2, keepdims=False
    ).reshape(out_rows, -1)
    out_slice = lax.all_gather(out_own, "fsdp", axis=0, tiled=True)
    own_units = left_weight.shape[0] // size
    hidden = lambda weight: lax.dynamic_slice_in_dim(weight, me_seq * own_units, own_units, 0)
    sides = lax.all_gather(
        jnp.concatenate([hidden(left_weight), hidden(right_weight)], 1), "fsdp", axis=0, tiled=True
    )
    left_slice, right_slice = sides[:, :feat], sides[:, feat:]
    down_slice = lax.all_gather(hidden(down_weight), "fsdp", axis=0, tiled=True)

    normed_all = whole(spread(normed))

    positions = me_seq * slots + lax.iota(jnp.int32, slots)
    valid = [(positions < lengths[b]).astype(F32)[:, None] for b in span]
    grad_y = [v * cotangent[b].astype(F32) for b, v in zip(span, valid)]
    grad_all = whole(spread([g.astype(LOW) for g in grad_y]))

    heads = decay.shape[0]
    all_decay = lax.all_gather(decay, "seq", axis=0, tiled=True).reshape(heads, size, -1)
    own_decay = lax.dynamic_index_in_dim(all_decay, me_seq, 1, keepdims=False)
    across = jnp.cumsum(own_decay.reshape(heads, size, slots), axis=-1)
    down = jnp.broadcast_to(across[..., None], (heads, size, slots, HEAD))
    me = me_seq.astype(jnp.int32).reshape(1)

    pre = times_rows(normed_all, project).astype(LOW).reshape(size, seqs, slots, -1)
    ungated, attn, squares = attend(me, pre, down, across)

    branch_parts = [
        cut(times_rows(ungated[i].reshape(seqs * slots, -1), out_slice).astype(LOW))
        for i in range(size)
    ]
    branch_raw = collect(branch_parts)
    square = jnp.sum(squares, axis=-1)
    square_own = square[0]
    for i in range(1, size):
        square_own = square_own + swap_seq(square[i], i)
    factor_attn = lax.rsqrt(square_own / feat + EPS)
    residual = [w + b * factor_attn[n][:, None] for n, (w, b) in enumerate(zip(wide, branch_raw))]
    factor_resid = [norm_factor(r) for r in residual]
    resid_low = [(r * f).astype(LOW) for r, f in zip(residual, factor_resid)]
    resid_all = whole(spread(resid_low))

    grad_product = times_rows(grad_all, down_slice)
    left = times_rows(resid_all, left_slice)
    right = times_rows(resid_all, right_slice)
    product = (left * right).astype(LOW)
    grad_left = (grad_product * right).astype(LOW)
    grad_right = (grad_product * left).astype(LOW)
    count = seqs * slots
    piece = lambda rows, i: rows[i * count : (i + 1) * count]
    grad_hn = collect(
        [
            cut(
                (
                    times(piece(grad_left, i), left_slice)
                    + times(piece(grad_right, i), right_slice)
                ).astype(LOW)
            )
            for i in range(size)
        ]
    )
    ffn = collect(
        [cut(times(piece(product, i), down_slice).astype(LOW)) for i in range(size)]
    )
    layer_out = jnp.stack(
        [(v * (r + f)).astype(LOW) for v, r, f in zip(valid, residual, ffn)]
    )

    down_grad = rows_outer(product, grad_all).astype(LOW)
    left_grad = rows_outer(grad_left, resid_all).astype(LOW)
    right_grad = rows_outer(grad_right, resid_all).astype(LOW)

    def share(grad):
        own = lax.psum_scatter(grad, "fsdp", scatter_dimension=0, tiled=True)
        return place_rows(spread(halves(own)), me_seq)

    down_out = share(down_grad)
    left_out = share(left_grad)
    right_out = share(right_grad)

    grad_resid = [
        g + norm_back(r, f, h) for g, r, f, h in zip(grad_y, residual, factor_resid, grad_hn)
    ]
    grad_branch = [g.astype(LOW) for g in grad_resid]
    branch_all = whole(spread(grad_branch))
    inner = jnp.stack(
        [jnp.mean(g.astype(F32) * b, axis=-1) for g, b in zip(grad_branch, branch_raw)]
    )
    scalars = jnp.stack([factor_attn, (factor_attn * inner) * factor_attn * factor_attn])
    scalars = jnp.stack([scalars] + [swap_seq(scalars, i) for i in range(1, size)])
    shape_scalars = (size, seqs, slots, HEAD)
    factor_cols = jnp.broadcast_to(scalars[:, 0, :, :, None], shape_scalars)
    inner_cols = jnp.broadcast_to(scalars[:, 1, :, :, None], shape_scalars)
    grad_gated = times(branch_all, out_slice).reshape(size, seqs, slots, -1)
    grad_pre, gated = attend_back(
        me, pre, attn, grad_gated, factor_cols, inner_cols, down, across
    )
    grad_pre_rows = grad_pre.reshape(rows_all, -1)
    grad_normed = collect(
        [cut(times(piece(grad_pre_rows, i), project).astype(LOW)) for i in range(size)]
    )
    input_grad = jnp.stack(
        [
            (g + norm_back(w, r, n)).astype(LOW)
            for g, w, r, n in zip(grad_resid, wide, factor_in, grad_normed)
        ]
    )
    project_grad = rows_outer(grad_pre_rows, normed_all).astype(LOW)
    out_grad = rows_outer(branch_all, gated.reshape(rows_all, -1)).astype(LOW)
    query_out, key_out, value_out, outgate_out = scatter_projections(
        project_grad, query_weight.shape[0], me_seq, me_fsdp
    )
    out_mine = lax.psum_scatter(out_grad, "fsdp", scatter_dimension=0, tiled=True)
    out_pieces = [jnp.concatenate(u, 0) for u in spread(halves(out_mine))]
    out_cols = in_order(out_pieces, me_seq)
    out_out = jnp.concatenate(
        [
            part[:, h * HEAD : (h + 1) * HEAD]
            for h in range(out_own.shape[1] // HEAD)
            for part in out_cols
        ],
        1,
    ).astype(F32)
    return (
        layer_out,
        input_grad,
        query_out,
        key_out,
        value_out,
        outgate_out,
        out_out,
        left_out,
        right_out,
        down_out,
    )


def solution(mesh):
    placed = (
        P("fsdp", "seq", None),
        P("fsdp", "seq", None),
        P("fsdp"),
        P("seq", None),
    ) + (P("fsdp", None),) * 8
    return jax.shard_map(
        on_device,
        mesh=mesh,
        in_specs=placed,
        out_specs=(P("fsdp", "seq", None),) * 2 + (P("fsdp", None),) * 8,
        check_vma=False,
    )
```

```python
import functools

import jax
import jax.numpy as jnp
from jax import lax
from jax.experimental import pallas as pl
from jax.experimental.pallas import tpu as pltpu
from jax.sharding import PartitionSpec as P

HEAD = 128
EPS = 1e-06
F32 = jnp.float32
LOW = jnp.bfloat16


def swap_seq(x, bit):
    size = lax.axis_size("seq")
    return lax.ppermute(x, "seq", [(i, i ^ bit) for i in range(size)])


def swap_core(x):
    size = lax.axis_size("fsdp")
    return lax.ppermute(x, "fsdp", [(i, i ^ 1) for i in range(size)])


def halfway(rows):
    return max(16, rows // 32 * 16)


def spread_near(x):
    size = lax.axis_size("seq")
    if size != 4:
        return [x] + [swap_seq(x, i) for i in range(1, size)]
    return [x, swap_seq(x, 1), swap_seq(x, 2)]


def spread_far(near):
    if len(near) != 3:
        return [[x] for x in near]
    _, by_x, by_y = near
    cut = halfway(by_x.shape[0])
    return [[x] for x in near] + [[swap_seq(by_x[:cut], 2), swap_seq(by_y[cut:], 1)]]


def spread(x):
    return spread_far(spread_near(x))


def collect_far(part):
    if lax.axis_size("seq") != 4:
        return ()
    cut = halfway(part.shape[0])
    return swap_seq(part[:cut], 1), swap_seq(part[cut:], 2)


def collect_near(parts, passed):
    wide = lambda x: x.astype(F32)
    if not passed:
        total = wide(parts[0])
        for i in range(1, len(parts)):
            total = total + wide(swap_seq(parts[i], i))
        return total
    by_x, by_y = passed
    cut = by_x.shape[0]
    to_x = lax.dynamic_update_slice_in_dim(
        parts[1], (wide(parts[1][cut:]) + wide(by_y)).astype(LOW), cut, 0
    )
    to_y = lax.dynamic_update_slice_in_dim(
        parts[2], (wide(parts[2][:cut]) + wide(by_x)).astype(LOW), 0, 0
    )
    return wide(parts[0]) + wide(swap_seq(to_x, 1)) + wide(swap_seq(to_y, 2))


def after(value, *others):
    return lax.optimization_barrier((value, others))[0]


def times_rows(left_side, weight):
    return lax.dot_general(
        left_side, weight, (((1,), (1,)), ((), ())), preferred_element_type=F32
    )


def times(left_side, weight):
    return lax.dot_general(
        left_side, weight, (((1,), (0,)), ((), ())), preferred_element_type=F32
    )


def rows_outer(left_side, right_side):
    return lax.dot_general(
        left_side, right_side, (((0,), (0,)), ((), ())), preferred_element_type=F32
    )


def norm_factor(values):
    return lax.rsqrt(jnp.mean(values * values, axis=-1, keepdims=True) + EPS)


def norm_back(values, factor, grad_in):
    inner_mean = jnp.mean(grad_in * values, axis=-1, keepdims=True)
    return factor * grad_in - values * (factor * factor * factor) * inner_mean


def sigmoid(x):
    return 1.0 / (1.0 + jnp.exp(-x))


def dot_nt(a, b):
    return lax.dot_general(a, b, (((1,), (1,)), ((), ())), preferred_element_type=F32)


def dot_nn(a, b):
    return lax.dot_general(a, b, (((1,), (0,)), ((), ())), preferred_element_type=F32)


def dot_tn(a, b):
    return lax.dot_general(a, b, (((0,), (0,)), ((), ())), preferred_element_type=F32)


def decay_weights(down, across):
    count = down.shape[0]
    rows = lax.broadcasted_iota(jnp.int32, (count, count), 0)
    cols = lax.broadcasted_iota(jnp.int32, (count, count), 1)
    apart = down[:, :1] - across
    return jnp.where(rows >= cols, jnp.exp(jnp.minimum(apart, 0.0)), 0.0)


def attend_kernel(s_ref, pre_ref, down_ref, across_ref, out_ref, attn_ref, square_ref, state_ref):
    me = s_ref[0]
    head = pl.program_id(1)
    blocks = pre_ref.shape[0]
    state_ref[...] = jnp.zeros_like(state_ref)

    def step(c, carry):
        i = lax.bitwise_xor(jnp.int32(c), me)
        pre_q = pre_ref[i, 0, :, 0:HEAD].astype(F32)
        pre_k = pre_ref[i, 0, :, HEAD : 2 * HEAD].astype(F32)
        value = pre_ref[i, 0, :, 2 * HEAD : 3 * HEAD]
        gate = pre_ref[i, 0, :, 3 * HEAD : 4 * HEAD].astype(F32)
        query = (pre_q * sigmoid(pre_q)).astype(LOW)
        key = pre_k * sigmoid(pre_k)
        down = down_ref[0, c]
        across = across_ref[0, pl.ds(c, 1), :]
        weights = decay_weights(down, across)
        scores = (dot_nt(query, key.astype(LOW)) * weights).astype(LOW)
        state = state_ref[...]
        out = dot_nn(scores, value) + dot_nn(query, state.astype(LOW)) * jnp.exp(down)
        last = down[down.shape[0] - 1 :, :]
        tail = (key * jnp.exp(last - down)).astype(LOW)
        state_ref[...] = jnp.exp(last) * state + dot_tn(tail, value)
        low = out.astype(LOW)
        attn_ref[i, 0] = low
        rounded = low.astype(F32)
        out_ref[i, 0] = (rounded * gate).astype(LOW)
        before = jnp.where(head == 0, 0.0, square_ref[i, 0])
        square_ref[i, 0] = before + rounded * rounded
        return carry

    lax.fori_loop(0, blocks, step, 0)


def attend_back_kernel(
    s_ref,
    pre_ref,
    attn_ref,
    grad_ref,
    inner_ref,
    down_ref,
    across_ref,
    out_ref,
    states_ref,
    state_ref,
):
    me = s_ref[0]
    blocks = pre_ref.shape[0]
    state_ref[...] = jnp.zeros_like(state_ref)

    def forward(c, carry):
        i = lax.bitwise_xor(jnp.int32(c), me)
        pre_k = pre_ref[i, 0, :, HEAD : 2 * HEAD].astype(F32)
        value = pre_ref[i, 0, :, 2 * HEAD : 3 * HEAD]
        key = pre_k * sigmoid(pre_k)
        down = down_ref[0, c]
        last = down[down.shape[0] - 1 :, :]
        tail = (key * jnp.exp(last - down)).astype(LOW)
        state = state_ref[...]
        states_ref[c] = state.astype(LOW)
        state_ref[...] = jnp.exp(last) * state + dot_tn(tail, value)
        return carry

    lax.fori_loop(0, blocks, forward, 0)
    state_ref[...] = jnp.zeros_like(state_ref)

    def backward(n, carry):
        c = blocks - 1 - n
        i = lax.bitwise_xor(jnp.int32(c), me)
        pre_q = pre_ref[i, 0, :, 0:HEAD].astype(F32)
        pre_k = pre_ref[i, 0, :, HEAD : 2 * HEAD].astype(F32)
        value = pre_ref[i, 0, :, 2 * HEAD : 3 * HEAD]
        gate = pre_ref[i, 0, :, 3 * HEAD : 4 * HEAD].astype(F32)
        attn = attn_ref[i, 0].astype(F32)
        grad = grad_ref[i, 0].astype(F32)
        grad_gate = grad * attn
        grad_attn = (grad * gate - attn * inner_ref[i, 0]).astype(LOW)
        sig_q = sigmoid(pre_q)
        sig_k = sigmoid(pre_k)
        query = pre_q * sig_q
        key = pre_k * sig_k
        query_low = query.astype(LOW)
        key_low = key.astype(LOW)
        down = down_ref[0, c]
        across = across_ref[0, pl.ds(c, 1), :]
        last = down[down.shape[0] - 1 :, :]
        weights = decay_weights(down, across)
        scores = (dot_nt(query_low, key_low) * weights).astype(LOW)
        paired = (dot_nt(grad_attn, value) * weights).astype(LOW)
        tail = jnp.exp(last - down)
        later = state_ref[...]
        later_low = later.astype(LOW)
        grown = jnp.exp(down)
        grad_q = dot_nn(paired, key_low) + grown * dot_nt(grad_attn, states_ref[c])
        grad_k = dot_tn(paired, query_low) + tail * dot_nt(value, later_low)
        grad_v = dot_tn(scores, grad_attn) + tail * dot_nn(key_low, later_low)
        state_ref[...] = jnp.exp(last) * later + dot_tn((query * grown).astype(LOW), grad_attn)
        out_ref[i, 0, :, 0:HEAD] = (grad_q * (sig_q * (1.0 + pre_q * (1.0 - sig_q)))).astype(LOW)
        out_ref[i, 0, :, HEAD : 2 * HEAD] = (
            grad_k * (sig_k * (1.0 + pre_k * (1.0 - sig_k)))
        ).astype(LOW)
        out_ref[i, 0, :, 2 * HEAD : 3 * HEAD] = grad_v.astype(LOW)
        out_ref[i, 0, :, 3 * HEAD : 4 * HEAD] = grad_gate.astype(LOW)
        return carry

    lax.fori_loop(0, blocks, backward, 0)


def attend(me, pre, down, across):
    blocks, seqs, slots, width = pre.shape
    heads = width // (4 * HEAD)
    one = pl.BlockSpec((blocks, 1, slots, HEAD), lambda b, h, s: (0, b, 0, h))
    return pl.pallas_call(
        attend_kernel,
        grid_spec=pltpu.PrefetchScalarGridSpec(
            num_scalar_prefetch=1,
            grid=(seqs, heads),
            in_specs=[
                pl.BlockSpec((blocks, 1, slots, 4 * HEAD), lambda b, h, s: (0, b, 0, h)),
                pl.BlockSpec((1, blocks, slots, HEAD), lambda b, h, s: (h, 0, 0, 0)),
                pl.BlockSpec((1, blocks, slots), lambda b, h, s: (h, 0, 0)),
            ],
            out_specs=[
                one,
                one,
                pl.BlockSpec((blocks, 1, slots, HEAD), lambda b, h, s: (0, b, 0, 0)),
            ],
            scratch_shapes=[pltpu.VMEM((HEAD, HEAD), F32)],
        ),
        out_shape=[
            jax.ShapeDtypeStruct((blocks, seqs, slots, heads * HEAD), LOW),
            jax.ShapeDtypeStruct((blocks, seqs, slots, heads * HEAD), LOW),
            jax.ShapeDtypeStruct((blocks, seqs, slots, HEAD), F32),
        ],
        compiler_params=pltpu.CompilerParams(
            dimension_semantics=("arbitrary", "arbitrary"), vmem_limit_bytes=32 << 20
        ),
        cost_estimate=pl.CostEstimate(
            flops=2_500_000_000, bytes_accessed=16 << 20, transcendentals=4_000_000
        ),
        name="attend",
    )(me, pre, down, across)


def attend_back(me, pre, attn, grad, inner, down, across):
    blocks, seqs, slots, width = pre.shape
    heads = width // (4 * HEAD)
    one = pl.BlockSpec((blocks, 1, slots, HEAD), lambda b, h, s: (0, b, 0, h))
    four = pl.BlockSpec((blocks, 1, slots, 4 * HEAD), lambda b, h, s: (0, b, 0, h))
    same = pl.BlockSpec((blocks, 1, slots, HEAD), lambda b, h, s: (0, b, 0, 0))
    return pl.pallas_call(
        attend_back_kernel,
        grid_spec=pltpu.PrefetchScalarGridSpec(
            num_scalar_prefetch=1,
            grid=(seqs, heads),
            in_specs=[
                four,
                one,
                one,
                same,
                pl.BlockSpec((1, blocks, slots, HEAD), lambda b, h, s: (h, 0, 0, 0)),
                pl.BlockSpec((1, blocks, slots), lambda b, h, s: (h, 0, 0)),
            ],
            out_specs=four,
            scratch_shapes=[
                pltpu.VMEM((blocks, HEAD, HEAD), LOW),
                pltpu.VMEM((HEAD, HEAD), F32),
            ],
        ),
        out_shape=jax.ShapeDtypeStruct((blocks, seqs, slots, width), LOW),
        compiler_params=pltpu.CompilerParams(
            dimension_semantics=("arbitrary", "arbitrary"), vmem_limit_bytes=40 << 20
        ),
        cost_estimate=pl.CostEstimate(
            flops=8_000_000_000, bytes_accessed=32 << 20, transcendentals=8_000_000
        ),
        name="attend_back",
    )(me, pre, attn, grad, inner, down, across)


CHUNK = 512


def chunks(hidden):
    full = hidden // CHUNK
    return [(c * CHUNK, CHUNK) for c in range(full)] + (
        [(full * CHUNK, hidden % CHUNK)] if hidden % CHUNK else []
    )


def each_chunk(hidden, step):
    full = hidden // CHUNK

    def body(c, carry):
        step(c, pl.multiple_of(c * CHUNK, CHUNK), CHUNK)
        return carry

    lax.fori_loop(0, full, body, 0)
    if hidden % CHUNK:
        step(full, full * CHUNK, hidden % CHUNK)


def row_copies(sources, to, sem, first):
    copies, start = [], 0
    for n, source in enumerate(sources):
        count = source.shape[0]
        copies.append(
            pltpu.make_async_copy(source, to.at[pl.ds(start, count)], sem.at[first + n])
        )
        start += count
    return copies


def unit_forward_kernel(piece, inputs, refs_in, *refs):
    rows = refs[:inputs]
    sides = refs[inputs]
    kept = refs[refs_in : refs_in + 3]
    xs, left, right, low_left, low_right, prod, row_sem, side_sem, out_sem = refs[refs_in + 3 :]
    hidden, feat = left.shape

    def fetch(c, start, length):
        here = pl.ds(start, length)
        return [
            pltpu.make_async_copy(sides.at[here, pl.ds(0, feat)], left.at[here], side_sem.at[0, c]),
            pltpu.make_async_copy(
                sides.at[here, pl.ds(feat, feat)], right.at[here], side_sem.at[1, c]
            ),
        ]

    def store(c, start, length):
        here = pl.ds(start, length)
        return [
            pltpu.make_async_copy(source.at[:, here], to.at[piece, :, here], out_sem.at[k, c])
            for k, (source, to) in enumerate(zip((low_left, low_right, prod), kept))
        ]

    loads = row_copies(rows, xs, row_sem, 0)
    for copy in loads:
        copy.start()
    for c, (start, length) in enumerate(chunks(hidden)):
        for copy in fetch(c, start, length):
            copy.start()
    for copy in loads:
        copy.wait()

    def step(c, start, length):
        for copy in fetch(c, start, length):
            copy.wait()
        here = pl.ds(start, length)
        lefts = dot_nt(xs[...], left[here])
        rights = dot_nt(xs[...], right[here])
        low_left[:, here] = lefts.astype(LOW)
        low_right[:, here] = rights.astype(LOW)
        prod[:, here] = (lefts * rights).astype(LOW)
        for copy in store(c, start, length):
            copy.start()

    each_chunk(hidden, step)
    for c, (start, length) in enumerate(chunks(hidden)):
        for copy in store(c, start, length):
            copy.wait()


WIDE = 2048


def unit_backward_kernel(piece, inputs, refs_in, *refs):
    rows = refs[:inputs]
    sides, down_ref = refs[inputs : inputs + 2]
    saved = refs[inputs + 2 : inputs + 5]
    kept = refs[refs_in : refs_in + 2]
    head_ref, out_ref = refs[refs_in + 2 : refs_in + 4]
    gs, left, right, down, low_left, low_right, prod, gl, gr, hs, fs = refs[refs_in + 4 : -5]
    row_sem, down_sem, side_sem, prod_sem, out_sem = refs[-5:]
    hidden, feat = left.shape
    spans = [(n, n * WIDE) for n in range(feat // WIDE)]

    def fetch(c, start, length):
        here = pl.ds(start, length)
        return [pltpu.make_async_copy(down_ref.at[here], down.at[here], down_sem.at[0, c])] + [
            pltpu.make_async_copy(source.at[piece, :, here], to.at[:, here], down_sem.at[1 + k, c])
            for k, (source, to) in enumerate(zip(saved[:2], (low_left, low_right)))
        ]

    def fetch_sides(n, start):
        return [
            pltpu.make_async_copy(
                sides.at[:, pl.ds(k * feat + start, WIDE)],
                to.at[:, pl.ds(start, WIDE)],
                side_sem.at[k, n],
            )
            for k, to in enumerate((left, right))
        ]

    def store(c, start, length):
        here = pl.ds(start, length)
        return [
            pltpu.make_async_copy(source.at[:, here], to.at[piece, :, here], out_sem.at[k, c])
            for k, (source, to) in enumerate(zip((gl, gr), kept))
        ]

    def store_wide(k, n, start):
        source, to = ((hs, head_ref), (fs, out_ref))[k]
        here = pl.ds(start, WIDE)
        return pltpu.make_async_copy(source.at[:, here], to.at[:, here], out_sem.at[2 + k, n])

    loads = row_copies(rows, gs, row_sem, 0)
    load_prod = pltpu.make_async_copy(saved[2].at[piece], prod, prod_sem)
    for copy in loads:
        copy.start()
    for c, (start, length) in enumerate(chunks(hidden)):
        for copy in fetch(c, start, length):
            copy.start()
    load_prod.start()
    for n, start in spans:
        for copy in fetch_sides(n, start):
            copy.start()
    for copy in loads:
        copy.wait()

    def step(c, start, length):
        for copy in fetch(c, start, length):
            copy.wait()
        here = pl.ds(start, length)
        grad = dot_nt(gs[...], down[here])
        gl[:, here] = (grad * low_right[:, here].astype(F32)).astype(LOW)
        gr[:, here] = (grad * low_left[:, here].astype(F32)).astype(LOW)
        for copy in store(c, start, length):
            copy.start()

    each_chunk(hidden, step)
    load_prod.wait()

    def outs(n, carry):
        start = pl.multiple_of(n * WIDE, WIDE)
        here = pl.ds(start, WIDE)
        fs[:, here] = dot_nn(prod[...], down[:, here]).astype(LOW)
        store_wide(1, n, start).start()
        return carry

    lax.fori_loop(0, len(spans), outs, 0)

    def heads(n, carry):
        start = pl.multiple_of(n * WIDE, WIDE)
        here = pl.ds(start, WIDE)
        for copy in fetch_sides(n, start):
            copy.wait()
        hs[:, here] = (dot_nn(gl[...], left[:, here]) + dot_nn(gr[...], right[:, here])).astype(LOW)
        store_wide(0, n, start).start()
        return carry

    lax.fori_loop(0, len(spans), heads, 0)
    for c, (start, length) in enumerate(chunks(hidden)):
        for copy in store(c, start, length):
            copy.wait()
    for n, start in spans:
        store_wide(1, n, start).wait()
        store_wide(0, n, start).wait()


def unit_forward(piece, size, rows, sides, kept):
    count = sum(r.shape[0] for r in rows)
    hidden, feat = sides.shape[0], sides.shape[1] // 2
    parts = len(chunks(hidden))
    anywhere = pl.BlockSpec(memory_space=pl.ANY)
    inputs = [*rows, sides]
    aliases = {}
    if kept is not None:
        aliases = {len(inputs) + k: k for k in range(3)}
        inputs += kept
    return pl.pallas_call(
        functools.partial(unit_forward_kernel, piece, len(rows), len(inputs)),
        in_specs=[anywhere] * len(inputs),
        out_specs=[anywhere] * 3,
        out_shape=[jax.ShapeDtypeStruct((size, count, hidden), LOW)] * 3,
        input_output_aliases=aliases,
        scratch_shapes=[
            pltpu.VMEM((count, feat), LOW),
            pltpu.VMEM((hidden, feat), LOW),
            pltpu.VMEM((hidden, feat), LOW),
            pltpu.VMEM((count, hidden), LOW),
            pltpu.VMEM((count, hidden), LOW),
            pltpu.VMEM((count, hidden), LOW),
            pltpu.SemaphoreType.DMA((len(rows),)),
            pltpu.SemaphoreType.DMA((2, parts)),
            pltpu.SemaphoreType.DMA((3, parts)),
        ],
        compiler_params=pltpu.CompilerParams(vmem_limit_bytes=40 << 20),
        cost_estimate=pl.CostEstimate(
            flops=4 * count * feat * hidden,
            bytes_accessed=2 * (2 * feat * hidden + count * (feat + 3 * hidden)),
            transcendentals=0,
        ),
        name="unit_forward",
    )(*inputs)


def unit_backward(piece, size, rows, sides, down, saved, kept):
    count = sum(r.shape[0] for r in rows)
    hidden, feat = down.shape
    parts = len(chunks(hidden))
    anywhere = pl.BlockSpec(memory_space=pl.ANY)
    inputs = [*rows, sides, down, *saved]
    aliases = {}
    if kept is not None:
        aliases = {len(inputs) + k: k for k in range(2)}
        inputs += kept
    wide = pltpu.VMEM((count, feat), LOW)
    side = pltpu.VMEM((hidden, feat), LOW)
    inner = pltpu.VMEM((count, hidden), LOW)
    outs = pl.pallas_call(
        functools.partial(unit_backward_kernel, piece, len(rows), len(inputs)),
        in_specs=[anywhere] * len(inputs),
        out_specs=[anywhere] * 4,
        out_shape=[jax.ShapeDtypeStruct((size, count, hidden), LOW)] * 2
        + [jax.ShapeDtypeStruct((count, feat), LOW)] * 2,
        input_output_aliases=aliases,
        scratch_shapes=[
            wide,
            side,
            side,
            side,
            inner,
            inner,
            inner,
            inner,
            inner,
            wide,
            wide,
            pltpu.SemaphoreType.DMA((len(rows),)),
            pltpu.SemaphoreType.DMA((3, parts)),
            pltpu.SemaphoreType.DMA((2, feat // WIDE)),
            pltpu.SemaphoreType.DMA,
            pltpu.SemaphoreType.DMA((4, max(parts, feat // WIDE))),
        ],
        compiler_params=pltpu.CompilerParams(vmem_limit_bytes=50 << 20),
        cost_estimate=pl.CostEstimate(
            flops=8 * count * feat * hidden,
            bytes_accessed=2 * (3 * feat * hidden + count * (3 * feat + 5 * hidden)),
            transcendentals=0,
        ),
        name="unit_backward",
    )(*inputs)
    return outs[:2], outs[2], outs[3]


def paired_heads(rows):
    return rows % HEAD == 0 and 2 * rows // HEAD == lax.axis_size("seq") == 4


def gather_projections(weights, me_seq, me_fsdp, meanwhile):
    rows, feat = weights[0].shape
    size = lax.axis_size("seq")
    if not paired_heads(rows):
        picked = []
        for weight in weights:
            full = lax.all_gather(weight, "fsdp", axis=0, tiled=True)
            full = full.reshape(-1, size, HEAD, feat)
            picked.append(lax.dynamic_index_in_dim(full, me_seq, 1, keepdims=False))
        return jnp.stack(picked, 1).reshape(-1, feat)
    core = me_fsdp % 2
    own = [
        lax.dynamic_slice_in_dim(weight, (me_seq % 2) * HEAD, HEAD, 0) for weight in weights
    ]
    first = jnp.concatenate(own[:2], 0)
    second = jnp.concatenate(own[2:], 0)
    keep = jnp.where(core == 0, first, second)
    give = jnp.where(core == 0, second, first)
    got = after(swap_core(give), meanwhile)
    return lax.all_gather(
        jnp.where(core == me_seq // 2, keep, got), "fsdp", axis=0, tiled=True
    )


def scatter_projections(grad, rows, me_seq, me_fsdp):
    feat = grad.shape[1]
    size = lax.axis_size("seq")
    if not paired_heads(rows):
        parts = grad.reshape(-1, 1, 4, HEAD, feat)
        result = []
        for which in range(4):
            full = jnp.zeros((parts.shape[0], size, HEAD, feat), grad.dtype)
            full = lax.dynamic_update_slice_in_dim(full, parts[:, :, which], me_seq, 1)
            part = lax.psum_scatter(
                full.reshape(-1, feat), "fsdp", scatter_dimension=0, tiled=True
            )
            result.append(lax.psum(part, "seq").astype(F32))
        return result
    core = me_fsdp % 2
    pieces = [jnp.concatenate(p, 0) for p in spread(grad)]
    straight = (core ^ (me_seq // 2)) == 0
    keep = [jnp.where(straight, pieces[j], pieces[2 + j]) for j in range(2)]
    give = [jnp.where(straight, pieces[2 + j], pieces[j]) for j in range(2)]
    got = [swap_core(g) for g in give]
    even = me_seq % 2 == 0
    keep = [jnp.where(even, keep[0], keep[1]), jnp.where(even, keep[1], keep[0])]
    got = [jnp.where(even, got[0], got[1]), jnp.where(even, got[1], got[0])]
    first = [jnp.where(core == 0, k, g) for k, g in zip(keep, got)]
    second = [jnp.where(core == 0, g, k) for k, g in zip(keep, got)]
    result = []
    for pair in (first, second):
        for part in range(2):
            span = slice(part * HEAD, (part + 1) * HEAD)
            result.append(jnp.concatenate([p[span] for p in pair], 0).astype(F32))
    return result


def in_order(pieces, me_seq):
    size = len(pieces)
    stack = jnp.stack(pieces)
    bit = 1
    index = lax.iota(jnp.int32, size)
    while bit < size:
        turned = jnp.stack([stack[i ^ bit] for i in range(size)])
        stack = jnp.where((me_seq & bit) != 0, turned, stack)
        bit *= 2
    return [stack[i] for i in range(size)]


def place_rows(pieces, me_seq, count):
    pieces = [jnp.concatenate(p, 0) if len(p) > 1 else p[0] for p in pieces]
    rows, feat = pieces[0].shape
    rows //= count
    result = []
    for n in range(count):
        out = jnp.zeros((rows * len(pieces), feat), F32)
        for i, piece in enumerate(pieces):
            out = lax.dynamic_update_slice_in_dim(
                out, piece[n * rows : (n + 1) * rows].astype(F32), (me_seq ^ i) * rows, 0
            )
        result.append(out)
    return result


def on_device(
    tokens,
    cotangent,
    lengths,
    decay,
    query_weight,
    key_weight,
    value_weight,
    outgate_weight,
    output_weight,
    left_weight,
    right_weight,
    down_weight,
):
    seqs, slots, feat = tokens.shape
    size = lax.axis_size("seq")
    me_seq = lax.axis_index("seq")
    me_fsdp = lax.axis_index("fsdp")
    count = seqs * slots
    rows_all = size * count

    def whole(pieces):
        return jnp.concatenate([part for parts in pieces for part in parts], 0)

    def cut(rows, i):
        return rows[i * count : (i + 1) * count]


    wide = tokens.reshape(count, feat).astype(F32)
    factor_in = norm_factor(wide)
    normed = (wide * factor_in).astype(LOW)
    normed_pieces = spread(normed)
    normed_all = whole(normed_pieces)

    project = gather_projections(
        (query_weight, key_weight, value_weight, outgate_weight), me_seq, me_fsdp, normed
    )
    out_rows = output_weight.shape[0]
    out_own = lax.dynamic_index_in_dim(
        output_weight.reshape(out_rows, -1, size, HEAD), me_seq, 2, keepdims=False
    ).reshape(out_rows, -1)
    out_slice = lax.all_gather(out_own, "fsdp", axis=0, tiled=True)
    own_units = left_weight.shape[0] // size
    hidden = lambda weight: lax.dynamic_slice_in_dim(weight, me_seq * own_units, own_units, 0)
    sides = lax.all_gather(
        jnp.concatenate([hidden(left_weight), hidden(right_weight)], 1), "fsdp", axis=0, tiled=True
    )
    down_slice = lax.all_gather(hidden(down_weight), "fsdp", axis=0, tiled=True)

    positions = me_seq * slots + lax.iota(jnp.int32, slots)
    valid = (positions[None, :] < lengths[:, None]).astype(F32).reshape(count, 1)
    grad_y = valid * cotangent.reshape(count, feat).astype(F32)
    grad_near = spread_near(after(grad_y.astype(LOW), normed_pieces[-1]))

    heads, slot_count = decay.shape
    if heads == size:
        send = lambda i: lax.dynamic_slice_in_dim(decay, me_seq ^ i, 1, 0)
        own_decay = jnp.concatenate(
            in_order([send(0)] + [swap_seq(send(i), i) for i in range(1, size)], me_seq), 0
        )
    else:
        all_decay = lax.all_gather(decay, "seq", axis=0, tiled=True).reshape(heads, size, -1)
        own_decay = lax.dynamic_index_in_dim(all_decay, me_seq, 1, keepdims=False)
    across = jnp.cumsum(own_decay.reshape(heads, size, slots), axis=-1)
    down = jnp.broadcast_to(across[..., None], (heads, size, slots, HEAD))
    me = me_seq.astype(jnp.int32).reshape(1)

    pre = times_rows(normed_all, project).astype(LOW).reshape(size, seqs, slots, -1)
    ungated, attn, squares = attend(me, pre, down, across)
    ungated = after(ungated.reshape(rows_all, -1), grad_near[1:])
    branch = lambda i: times_rows(cut(ungated, i), out_slice).astype(LOW)
    branch_parts = [None] * (size - 1) + [branch(size - 1)]
    branch_far = collect_far(branch_parts[-1])
    for i in reversed(range(size - 1)):
        branch_parts[i] = branch(i)
    branch_raw = collect_near(branch_parts, branch_far)
    square = jnp.sum(squares, axis=-1).reshape(size, count)
    square_own = square[0]
    for i in range(1, size):
        square_own = square_own + swap_seq(square[i], i)
    factor_attn = lax.rsqrt(square_own / feat + EPS)[:, None]
    residual = wide + branch_raw * factor_attn
    factor_resid = norm_factor(residual)
    resid_pieces = spread((residual * factor_resid).astype(LOW))
    resid_all = whole(resid_pieces)
    grad_pieces = spread_far(after(grad_near, resid_pieces[-1]))
    grad_all = whole(grad_pieces)

    def own_rows(grad):
        return lax.psum_scatter(grad, "fsdp", scatter_dimension=0, tiled=True)

    saved = None
    for i in range(size):
        saved = unit_forward(i, size, resid_pieces[i], sides, saved)
    down_grad = rows_outer(saved[2].reshape(rows_all, -1), grad_all).astype(LOW)
    down_mine = own_rows(down_grad)
    head_parts, ffn_parts = [None] * size, [None] * size

    def back(i, rows, kept):
        kept, head_parts[i], ffn_parts[i] = unit_backward(
            i, size, rows, sides, down_slice, saved, kept
        )
        return kept

    kept = back(size - 1, after(grad_pieces[-1], down_grad), None)
    head_far = collect_far(head_parts[-1])
    ffn_far = collect_far(ffn_parts[-1])
    for i in range(1, size - 1):
        kept = back(i, grad_pieces[i], kept)
    kept = back(0, after(grad_pieces[0], head_far, ffn_far), kept)
    grad_hn = collect_near(head_parts, head_far)
    grad_left, grad_right = [k.reshape(rows_all, -1) for k in kept]
    left_grad = rows_outer(grad_left, resid_all).astype(LOW)
    left_mine = own_rows(left_grad)
    grad_hn = after(grad_hn, left_grad)

    grad_resid = grad_y + norm_back(residual, factor_resid, grad_hn)
    grad_branch = (grad_resid * factor_attn).astype(LOW)
    branch_near = spread_near(grad_branch)
    right_grad = rows_outer(after(grad_right, grad_branch), resid_all).astype(LOW)
    right_mine = own_rows(right_grad)
    inner = jnp.mean(grad_branch.astype(F32) * branch_raw, axis=-1, keepdims=True)
    inner = (inner * factor_attn * factor_attn)[:, 0]
    inner = jnp.stack([inner] + [swap_seq(inner, i) for i in range(1, size)])
    inner = jnp.broadcast_to(inner.reshape(size, seqs, slots, 1), (size, seqs, slots, HEAD))
    branch_near = after(branch_near, right_grad)
    branch_pieces = spread_far(branch_near)
    branch_all = whole(branch_pieces)
    grad_gated = times(branch_all, out_slice).reshape(size, seqs, slots, -1)

    grad_pre = attend_back(me, pre, attn, grad_gated, inner, down, across)
    ffn = collect_near([ffn_parts[0]] + after(ffn_parts[1:], branch_pieces[-1]), ffn_far)
    grad_pre = after(grad_pre.reshape(rows_all, -1), ffn, down_mine)
    out_grad = rows_outer(branch_all, after(ungated, grad_pre)).astype(LOW)
    out_mine = own_rows(after(out_grad, right_mine))
    project_grad = rows_outer(after(grad_pre, out_grad), normed_all).astype(LOW)
    project_mine = own_rows(project_grad) if paired_heads(query_weight.shape[0]) else project_grad
    layer_out = (valid * (residual + ffn)).astype(LOW).reshape(tokens.shape)

    down_near = spread_near(after(down_mine, ffn))
    normed_part = lambda i, rows: times(cut(rows, i), project).astype(LOW)
    normed_parts = [None] * (size - 1) + [normed_part(size - 1, after(grad_pre, project_grad, down_near))]
    normed_far = collect_far(after(normed_parts[-1], left_mine))
    for i in reversed(range(size - 1)):
        normed_parts[i] = normed_part(i, after(grad_pre, normed_parts[-1]))
    grad_normed = collect_near(normed_parts, normed_far)
    sides_near = spread_near(after(jnp.concatenate([left_mine, right_mine], 0), ffn))
    grad_normed = after(grad_normed, sides_near, out_mine, project_mine)
    input_grad = grad_resid + norm_back(wide, factor_in, grad_normed)
    input_grad = input_grad.astype(LOW).reshape(tokens.shape)

    (down_out,) = place_rows(spread_far(down_near), me_seq, 1)
    left_out, right_out = place_rows(spread_far(sides_near), me_seq, 2)

    query_out, key_out, value_out, outgate_out = scatter_projections(
        project_mine, query_weight.shape[0], me_seq, me_fsdp
    )
    out_pieces = [jnp.concatenate(p, 0) for p in spread(out_mine)]
    out_cols = in_order(out_pieces, me_seq)
    out_out = jnp.concatenate(
        [
            part[:, h * HEAD : (h + 1) * HEAD]
            for h in range(out_own.shape[1] // HEAD)
            for part in out_cols
        ],
        1,
    ).astype(F32)
    return (
        layer_out,
        input_grad,
        query_out,
        key_out,
        value_out,
        outgate_out,
        out_out,
        left_out,
        right_out,
        down_out,
    )


def solution(mesh):
    placed = (
        P("fsdp", "seq", None),
        P("fsdp", "seq", None),
        P("fsdp"),
        P("seq", None),
    ) + (P("fsdp", None),) * 8
    return jax.shard_map(
        on_device,
        mesh=mesh,
        in_specs=placed,
        out_specs=(P("fsdp", "seq", None),) * 2 + (P("fsdp", None),) * 8,
        check_vma=False,
    )
```

```python
import functools

import jax
import jax.numpy as jnp
from jax import lax
from jax.experimental import pallas as pl
from jax.experimental.pallas import tpu as pltpu
from jax.sharding import PartitionSpec as P

HEAD = 128
EPS = 1e-06
F32 = jnp.float32
LOW = jnp.bfloat16


def swap_seq(x, bit):
    size = lax.axis_size("seq")
    return lax.ppermute(x, "seq", [(i, i ^ bit) for i in range(size)])


def swap_core(x):
    size = lax.axis_size("fsdp")
    return lax.ppermute(x, "fsdp", [(i, i ^ 1) for i in range(size)])


def halfway(rows):
    return max(16, rows // 32 * 16)


def spread_near(x):
    size = lax.axis_size("seq")
    if size != 4:
        return [x] + [swap_seq(x, i) for i in range(1, size)]
    return [x, swap_seq(x, 1), swap_seq(x, 2)]


def spread_far(near):
    if len(near) != 3:
        return [[x] for x in near]
    _, by_x, by_y = near
    cut = halfway(by_x.shape[0])
    return [[x] for x in near] + [[swap_seq(by_x[:cut], 2), swap_seq(by_y[cut:], 1)]]


def spread(x):
    return spread_far(spread_near(x))


def halves(rows):
    cut = halfway(rows)
    return [slice(0, cut), slice(cut, rows)] if lax.axis_size("seq") == 4 else [slice(0, rows)]


def collect_far(part):
    if lax.axis_size("seq") != 4:
        return ()
    top, rest = part
    return swap_seq(top, 1), swap_seq(rest, 2)


def join_near(parts, passed):
    wide = lambda x: x.astype(F32)
    if not passed:
        return [part[0] if isinstance(part, list) else part for part in parts[1:]]
    by_x, by_y = passed
    cut = by_x.shape[0]
    to_x = lax.dynamic_update_slice_in_dim(
        parts[1], (wide(parts[1][cut:]) + wide(by_y)).astype(LOW), cut, 0
    )
    to_y = lax.dynamic_update_slice_in_dim(
        parts[2], (wide(parts[2][:cut]) + wide(by_x)).astype(LOW), 0, 0
    )
    return [to_x, to_y]


def collect_joined(own, joined):
    total = own.astype(F32)
    for i, part in enumerate(joined):
        total = total + swap_seq(part, i + 1).astype(F32)
    return total


def collect_near(parts, passed):
    return collect_joined(parts[0], join_near(parts, passed))


def after(value, *others):
    return lax.optimization_barrier((value, others))[0]


def times_rows(left_side, weight):
    return lax.dot_general(
        left_side, weight, (((1,), (1,)), ((), ())), preferred_element_type=F32
    )


def times(left_side, weight):
    return lax.dot_general(
        left_side, weight, (((1,), (0,)), ((), ())), preferred_element_type=F32
    )


def rows_outer(left_side, right_side):
    return lax.dot_general(
        left_side, right_side, (((0,), (0,)), ((), ())), preferred_element_type=F32
    )


def norm_factor(values):
    return lax.rsqrt(jnp.mean(values * values, axis=-1, keepdims=True) + EPS)


def norm_back(values, factor, grad_in):
    inner_mean = jnp.mean(grad_in * values, axis=-1, keepdims=True)
    return factor * grad_in - values * (factor * factor * factor) * inner_mean


def sigmoid(x):
    return 1.0 / (1.0 + jnp.exp(-x))


def dot_nt(a, b):
    return lax.dot_general(a, b, (((1,), (1,)), ((), ())), preferred_element_type=F32)


def dot_nn(a, b):
    return lax.dot_general(a, b, (((1,), (0,)), ((), ())), preferred_element_type=F32)


def dot_tn(a, b):
    return lax.dot_general(a, b, (((0,), (0,)), ((), ())), preferred_element_type=F32)


def decay_weights(down, across):
    count = down.shape[0]
    rows = lax.broadcasted_iota(jnp.int32, (count, count), 0)
    cols = lax.broadcasted_iota(jnp.int32, (count, count), 1)
    apart = down[:, :1] - across
    return jnp.where(rows >= cols, jnp.exp(jnp.minimum(apart, 0.0)), 0.0)


def attend_kernel(s_ref, pre_ref, down_ref, across_ref, out_ref, attn_ref, square_ref, state_ref):
    me = s_ref[0]
    head = pl.program_id(1)
    blocks = pre_ref.shape[0]
    state_ref[...] = jnp.zeros_like(state_ref)

    def step(c, carry):
        i = lax.bitwise_xor(jnp.int32(c), me)
        pre_q = pre_ref[i, 0, :, 0:HEAD].astype(F32)
        pre_k = pre_ref[i, 0, :, HEAD : 2 * HEAD].astype(F32)
        value = pre_ref[i, 0, :, 2 * HEAD : 3 * HEAD]
        gate = pre_ref[i, 0, :, 3 * HEAD : 4 * HEAD].astype(F32)
        query = (pre_q * sigmoid(pre_q)).astype(LOW)
        key = pre_k * sigmoid(pre_k)
        down = down_ref[0, c]
        across = across_ref[0, pl.ds(c, 1), :]
        weights = decay_weights(down, across)
        scores = (dot_nt(query, key.astype(LOW)) * weights).astype(LOW)
        state = state_ref[...]
        out = dot_nn(scores, value) + dot_nn(query, state.astype(LOW)) * jnp.exp(down)
        last = down[down.shape[0] - 1 :, :]
        tail = (key * jnp.exp(last - down)).astype(LOW)
        state_ref[...] = jnp.exp(last) * state + dot_tn(tail, value)
        low = out.astype(LOW)
        attn_ref[i, 0] = low
        rounded = low.astype(F32)
        out_ref[i, 0] = (rounded * gate).astype(LOW)
        before = jnp.where(head == 0, 0.0, square_ref[i, 0])
        square_ref[i, 0] = before + rounded * rounded
        return carry

    lax.fori_loop(0, blocks, step, 0)


def attend_back_kernel(
    s_ref,
    pre_ref,
    attn_ref,
    grad_ref,
    inner_ref,
    down_ref,
    across_ref,
    out_ref,
    states_ref,
    state_ref,
):
    me = s_ref[0]
    blocks = pre_ref.shape[0]
    state_ref[...] = jnp.zeros_like(state_ref)

    def forward(c, carry):
        i = lax.bitwise_xor(jnp.int32(c), me)
        pre_k = pre_ref[i, 0, :, HEAD : 2 * HEAD].astype(F32)
        value = pre_ref[i, 0, :, 2 * HEAD : 3 * HEAD]
        key = pre_k * sigmoid(pre_k)
        down = down_ref[0, c]
        last = down[down.shape[0] - 1 :, :]
        tail = (key * jnp.exp(last - down)).astype(LOW)
        state = state_ref[...]
        states_ref[c] = state.astype(LOW)
        state_ref[...] = jnp.exp(last) * state + dot_tn(tail, value)
        return carry

    lax.fori_loop(0, blocks, forward, 0)
    state_ref[...] = jnp.zeros_like(state_ref)

    def backward(n, carry):
        c = blocks - 1 - n
        i = lax.bitwise_xor(jnp.int32(c), me)
        pre_q = pre_ref[i, 0, :, 0:HEAD].astype(F32)
        pre_k = pre_ref[i, 0, :, HEAD : 2 * HEAD].astype(F32)
        value = pre_ref[i, 0, :, 2 * HEAD : 3 * HEAD]
        gate = pre_ref[i, 0, :, 3 * HEAD : 4 * HEAD].astype(F32)
        attn = attn_ref[i, 0].astype(F32)
        grad = grad_ref[i, 0].astype(F32)
        grad_gate = grad * attn
        grad_attn = (grad * gate - attn * inner_ref[i, 0]).astype(LOW)
        sig_q = sigmoid(pre_q)
        sig_k = sigmoid(pre_k)
        query = pre_q * sig_q
        key = pre_k * sig_k
        query_low = query.astype(LOW)
        key_low = key.astype(LOW)
        down = down_ref[0, c]
        across = across_ref[0, pl.ds(c, 1), :]
        last = down[down.shape[0] - 1 :, :]
        weights = decay_weights(down, across)
        scores = (dot_nt(query_low, key_low) * weights).astype(LOW)
        paired = (dot_nt(grad_attn, value) * weights).astype(LOW)
        tail = jnp.exp(last - down)
        later = state_ref[...]
        later_low = later.astype(LOW)
        grown = jnp.exp(down)
        grad_q = dot_nn(paired, key_low) + grown * dot_nt(grad_attn, states_ref[c])
        grad_k = dot_tn(paired, query_low) + tail * dot_nt(value, later_low)
        grad_v = dot_tn(scores, grad_attn) + tail * dot_nn(key_low, later_low)
        state_ref[...] = jnp.exp(last) * later + dot_tn((query * grown).astype(LOW), grad_attn)
        out_ref[i, 0, :, 0:HEAD] = (grad_q * (sig_q * (1.0 + pre_q * (1.0 - sig_q)))).astype(LOW)
        out_ref[i, 0, :, HEAD : 2 * HEAD] = (
            grad_k * (sig_k * (1.0 + pre_k * (1.0 - sig_k)))
        ).astype(LOW)
        out_ref[i, 0, :, 2 * HEAD : 3 * HEAD] = grad_v.astype(LOW)
        out_ref[i, 0, :, 3 * HEAD : 4 * HEAD] = grad_gate.astype(LOW)
        return carry

    lax.fori_loop(0, blocks, backward, 0)


def attend(me, pre, down, across):
    blocks, seqs, slots, width = pre.shape
    heads = width // (4 * HEAD)
    one = pl.BlockSpec((blocks, 1, slots, HEAD), lambda b, h, s: (0, b, 0, h))
    return pl.pallas_call(
        attend_kernel,
        grid_spec=pltpu.PrefetchScalarGridSpec(
            num_scalar_prefetch=1,
            grid=(seqs, heads),
            in_specs=[
                pl.BlockSpec((blocks, 1, slots, 4 * HEAD), lambda b, h, s: (0, b, 0, h)),
                pl.BlockSpec((1, blocks, slots, HEAD), lambda b, h, s: (h, 0, 0, 0)),
                pl.BlockSpec((1, blocks, slots), lambda b, h, s: (h, 0, 0)),
            ],
            out_specs=[
                one,
                one,
                pl.BlockSpec((blocks, 1, slots, HEAD), lambda b, h, s: (0, b, 0, 0)),
            ],
            scratch_shapes=[pltpu.VMEM((HEAD, HEAD), F32)],
        ),
        out_shape=[
            jax.ShapeDtypeStruct((blocks, seqs, slots, heads * HEAD), LOW),
            jax.ShapeDtypeStruct((blocks, seqs, slots, heads * HEAD), LOW),
            jax.ShapeDtypeStruct((blocks, seqs, slots, HEAD), F32),
        ],
        compiler_params=pltpu.CompilerParams(
            dimension_semantics=("arbitrary", "arbitrary"), vmem_limit_bytes=32 << 20
        ),
        cost_estimate=pl.CostEstimate(
            flops=2_500_000_000, bytes_accessed=16 << 20, transcendentals=4_000_000
        ),
        name="attend",
    )(me, pre, down, across)


def attend_back(me, pre, attn, grad, inner, down, across):
    blocks, seqs, slots, width = pre.shape
    heads = width // (4 * HEAD)
    one = pl.BlockSpec((blocks, 1, slots, HEAD), lambda b, h, s: (0, b, 0, h))
    four = pl.BlockSpec((blocks, 1, slots, 4 * HEAD), lambda b, h, s: (0, b, 0, h))
    same = pl.BlockSpec((blocks, 1, slots, HEAD), lambda b, h, s: (0, b, 0, 0))
    return pl.pallas_call(
        attend_back_kernel,
        grid_spec=pltpu.PrefetchScalarGridSpec(
            num_scalar_prefetch=1,
            grid=(seqs, heads),
            in_specs=[
                four,
                one,
                one,
                same,
                pl.BlockSpec((1, blocks, slots, HEAD), lambda b, h, s: (h, 0, 0, 0)),
                pl.BlockSpec((1, blocks, slots), lambda b, h, s: (h, 0, 0)),
            ],
            out_specs=four,
            scratch_shapes=[
                pltpu.VMEM((blocks, HEAD, HEAD), LOW),
                pltpu.VMEM((HEAD, HEAD), F32),
            ],
        ),
        out_shape=jax.ShapeDtypeStruct((blocks, seqs, slots, width), LOW),
        compiler_params=pltpu.CompilerParams(
            dimension_semantics=("arbitrary", "arbitrary"), vmem_limit_bytes=40 << 20
        ),
        cost_estimate=pl.CostEstimate(
            flops=8_000_000_000, bytes_accessed=32 << 20, transcendentals=8_000_000
        ),
        name="attend_back",
    )(me, pre, attn, grad, inner, down, across)


CHUNK = 512


def chunks(hidden):
    full = hidden // CHUNK
    return [(c * CHUNK, CHUNK) for c in range(full)] + (
        [(full * CHUNK, hidden % CHUNK)] if hidden % CHUNK else []
    )


def each_chunk(hidden, step):
    full = hidden // CHUNK

    def body(c, carry):
        step(c, pl.multiple_of(c * CHUNK, CHUNK), CHUNK)
        return carry

    lax.fori_loop(0, full, body, 0)
    if hidden % CHUNK:
        step(full, full * CHUNK, hidden % CHUNK)


def row_copies(sources, to, sem, first):
    copies, start = [], 0
    for n, source in enumerate(sources):
        count = source.shape[0]
        copies.append(
            pltpu.make_async_copy(source, to.at[pl.ds(start, count)], sem.at[first + n])
        )
        start += count
    return copies


def unit_forward_kernel(piece, inputs, refs_in, *refs):
    rows = refs[:inputs]
    sides = refs[inputs]
    kept = refs[refs_in : refs_in + 3]
    xs, left, right, low_left, low_right, prod, row_sem, side_sem, out_sem = refs[refs_in + 3 :]
    hidden, feat = left.shape

    def fetch(c, start, length):
        here = pl.ds(start, length)
        return [
            pltpu.make_async_copy(sides.at[here, pl.ds(0, feat)], left.at[here], side_sem.at[0, c]),
            pltpu.make_async_copy(
                sides.at[here, pl.ds(feat, feat)], right.at[here], side_sem.at[1, c]
            ),
        ]

    def store(c, start, length):
        here = pl.ds(start, length)
        return [
            pltpu.make_async_copy(source.at[:, here], to.at[piece, :, here], out_sem.at[k, c])
            for k, (source, to) in enumerate(zip((low_left, low_right, prod), kept))
        ]

    loads = row_copies(rows, xs, row_sem, 0)
    for copy in loads:
        copy.start()
    for c, (start, length) in enumerate(chunks(hidden)):
        for copy in fetch(c, start, length):
            copy.start()
    for copy in loads:
        copy.wait()

    def step(c, start, length):
        for copy in fetch(c, start, length):
            copy.wait()
        here = pl.ds(start, length)
        lefts = dot_nt(xs[...], left[here])
        rights = dot_nt(xs[...], right[here])
        low_left[:, here] = lefts.astype(LOW)
        low_right[:, here] = rights.astype(LOW)
        prod[:, here] = (lefts * rights).astype(LOW)
        for copy in store(c, start, length):
            copy.start()

    each_chunk(hidden, step)
    for c, (start, length) in enumerate(chunks(hidden)):
        for copy in store(c, start, length):
            copy.wait()


WIDE = 2048


def unit_backward_kernel(piece, inputs, refs_in, *refs):
    rows = refs[:inputs]
    sides, down_ref = refs[inputs : inputs + 2]
    saved = refs[inputs + 2 : inputs + 5]
    kept = refs[refs_in : refs_in + 2]
    outs = len(refs) - refs_in - 18
    head_refs = refs[refs_in + 2 : refs_in + 2 + outs // 2]
    out_refs = refs[refs_in + 2 + outs // 2 : refs_in + 2 + outs]
    gs, left, right, down, low_left, low_right, prod, gl, gr, hs, fs = refs[refs_in + 2 + outs : -5]
    row_sem, down_sem, side_sem, prod_sem, out_sem = refs[-5:]
    hidden, feat = left.shape
    spans = [(n, n * WIDE) for n in range(feat // WIDE)]

    def fetch(c, start, length):
        here = pl.ds(start, length)
        return [pltpu.make_async_copy(down_ref.at[here], down.at[here], down_sem.at[0, c])] + [
            pltpu.make_async_copy(source.at[piece, :, here], to.at[:, here], down_sem.at[1 + k, c])
            for k, (source, to) in enumerate(zip(saved[:2], (low_left, low_right)))
        ]

    def fetch_sides(n, start):
        return [
            pltpu.make_async_copy(
                sides.at[:, pl.ds(k * feat + start, WIDE)],
                to.at[:, pl.ds(start, WIDE)],
                side_sem.at[k, n],
            )
            for k, to in enumerate((left, right))
        ]

    def store(c, start, length):
        here = pl.ds(start, length)
        return [
            pltpu.make_async_copy(source.at[:, here], to.at[piece, :, here], out_sem.at[k, c])
            for k, (source, to) in enumerate(zip((gl, gr), kept))
        ]

    def store_wide(k, n, start):
        source, targets = ((hs, head_refs), (fs, out_refs))[k]
        here = pl.ds(start, WIDE)
        copies, first = [], 0
        for part, to in enumerate(targets):
            rows = pl.ds(first, to.shape[0])
            copies.append(
                pltpu.make_async_copy(
                    source.at[rows, here], to.at[:, here], out_sem.at[2 + 2 * k + part, n]
                )
            )
            first += to.shape[0]
        return copies

    loads = row_copies(rows, gs, row_sem, 0)
    load_prod = pltpu.make_async_copy(saved[2].at[piece], prod, prod_sem)
    for copy in loads:
        copy.start()
    for c, (start, length) in enumerate(chunks(hidden)):
        for copy in fetch(c, start, length):
            copy.start()
    load_prod.start()
    for n, start in spans:
        for copy in fetch_sides(n, start):
            copy.start()
    for copy in loads:
        copy.wait()

    def step(c, start, length):
        for copy in fetch(c, start, length):
            copy.wait()
        here = pl.ds(start, length)
        grad = dot_nt(gs[...], down[here])
        gl[:, here] = (grad * low_right[:, here].astype(F32)).astype(LOW)
        gr[:, here] = (grad * low_left[:, here].astype(F32)).astype(LOW)
        for copy in store(c, start, length):
            copy.start()

    each_chunk(hidden, step)
    load_prod.wait()

    def outs(n, carry):
        start = pl.multiple_of(n * WIDE, WIDE)
        here = pl.ds(start, WIDE)
        fs[:, here] = dot_nn(prod[...], down[:, here]).astype(LOW)
        for copy in store_wide(1, n, start):
            copy.start()
        return carry

    lax.fori_loop(0, len(spans), outs, 0)

    def heads(n, carry):
        start = pl.multiple_of(n * WIDE, WIDE)
        here = pl.ds(start, WIDE)
        for copy in fetch_sides(n, start):
            copy.wait()
        hs[:, here] = (dot_nn(gl[...], left[:, here]) + dot_nn(gr[...], right[:, here])).astype(LOW)
        for copy in store_wide(0, n, start):
            copy.start()
        return carry

    lax.fori_loop(0, len(spans), heads, 0)
    for c, (start, length) in enumerate(chunks(hidden)):
        for copy in store(c, start, length):
            copy.wait()
    for n, start in spans:
        for copy in store_wide(1, n, start) + store_wide(0, n, start):
            copy.wait()


def unit_forward(piece, size, rows, sides, kept):
    count = sum(r.shape[0] for r in rows)
    hidden, feat = sides.shape[0], sides.shape[1] // 2
    parts = len(chunks(hidden))
    anywhere = pl.BlockSpec(memory_space=pl.ANY)
    inputs = [*rows, sides]
    aliases = {}
    if kept is not None:
        aliases = {len(inputs) + k: k for k in range(3)}
        inputs += kept
    return pl.pallas_call(
        functools.partial(unit_forward_kernel, piece, len(rows), len(inputs)),
        in_specs=[anywhere] * len(inputs),
        out_specs=[anywhere] * 3,
        out_shape=[jax.ShapeDtypeStruct((size, count, hidden), LOW)] * 3,
        input_output_aliases=aliases,
        scratch_shapes=[
            pltpu.VMEM((count, feat), LOW),
            pltpu.VMEM((hidden, feat), LOW),
            pltpu.VMEM((hidden, feat), LOW),
            pltpu.VMEM((count, hidden), LOW),
            pltpu.VMEM((count, hidden), LOW),
            pltpu.VMEM((count, hidden), LOW),
            pltpu.SemaphoreType.DMA((len(rows),)),
            pltpu.SemaphoreType.DMA((2, parts)),
            pltpu.SemaphoreType.DMA((3, parts)),
        ],
        compiler_params=pltpu.CompilerParams(vmem_limit_bytes=40 << 20),
        cost_estimate=pl.CostEstimate(
            flops=4 * count * feat * hidden,
            bytes_accessed=2 * (2 * feat * hidden + count * (feat + 3 * hidden)),
            transcendentals=0,
        ),
        name="unit_forward",
    )(*inputs)


def unit_backward(piece, size, rows, sides, down, saved, kept):
    count = sum(r.shape[0] for r in rows)
    hidden, feat = down.shape
    parts = len(chunks(hidden))
    anywhere = pl.BlockSpec(memory_space=pl.ANY)
    inputs = [*rows, sides, down, *saved]
    aliases = {}
    if kept is not None:
        aliases = {len(inputs) + k: k for k in range(2)}
        inputs += kept
    wide = pltpu.VMEM((count, feat), LOW)
    side = pltpu.VMEM((hidden, feat), LOW)
    inner = pltpu.VMEM((count, hidden), LOW)
    spans = halves(count) if piece == size - 1 else [slice(0, count)]
    pieces = [jax.ShapeDtypeStruct((span.stop - span.start, feat), LOW) for span in spans]
    outs = pl.pallas_call(
        functools.partial(unit_backward_kernel, piece, len(rows), len(inputs)),
        in_specs=[anywhere] * len(inputs),
        out_specs=[anywhere] * (2 + 2 * len(pieces)),
        out_shape=[jax.ShapeDtypeStruct((size, count, hidden), LOW)] * 2 + pieces * 2,
        input_output_aliases=aliases,
        scratch_shapes=[
            wide,
            side,
            side,
            side,
            inner,
            inner,
            inner,
            inner,
            inner,
            wide,
            wide,
            pltpu.SemaphoreType.DMA((len(rows),)),
            pltpu.SemaphoreType.DMA((3, parts)),
            pltpu.SemaphoreType.DMA((2, feat // WIDE)),
            pltpu.SemaphoreType.DMA,
            pltpu.SemaphoreType.DMA((6, max(parts, feat // WIDE))),
        ],
        compiler_params=pltpu.CompilerParams(vmem_limit_bytes=50 << 20),
        cost_estimate=pl.CostEstimate(
            flops=8 * count * feat * hidden,
            bytes_accessed=2 * (3 * feat * hidden + count * (3 * feat + 5 * hidden)),
            transcendentals=0,
        ),
        name="unit_backward",
    )(*inputs)
    parts = [list(outs[2 : 2 + len(pieces)]), list(outs[2 + len(pieces) :])]
    return (outs[:2], *(part if piece == size - 1 else part[0] for part in parts))


def paired_heads(rows):
    return rows % HEAD == 0 and 2 * rows // HEAD == lax.axis_size("seq") == 4


def gather_projections(weights, me_seq, me_fsdp, meanwhile):
    rows, feat = weights[0].shape
    size = lax.axis_size("seq")
    if not paired_heads(rows):
        picked = []
        for weight in weights:
            full = lax.all_gather(weight, "fsdp", axis=0, tiled=True)
            full = full.reshape(-1, size, HEAD, feat)
            picked.append(lax.dynamic_index_in_dim(full, me_seq, 1, keepdims=False))
        return jnp.stack(picked, 1).reshape(-1, feat)
    core = me_fsdp % 2
    own = [
        lax.dynamic_slice_in_dim(weight, (me_seq % 2) * HEAD, HEAD, 0) for weight in weights
    ]
    first = jnp.concatenate(own[:2], 0)
    second = jnp.concatenate(own[2:], 0)
    keep = jnp.where(core == 0, first, second)
    give = jnp.where(core == 0, second, first)
    got = after(swap_core(give), meanwhile)
    return lax.all_gather(
        jnp.where(core == me_seq // 2, keep, got), "fsdp", axis=0, tiled=True
    )


def scatter_projections(grad, rows, me_seq, me_fsdp):
    size = lax.axis_size("seq")
    if not paired_heads(rows):
        feat = grad.shape[1]
        parts = grad.reshape(-1, 1, 4, HEAD, feat)
        result = []
        for which in range(4):
            full = jnp.zeros((parts.shape[0], size, HEAD, feat), grad.dtype)
            full = lax.dynamic_update_slice_in_dim(full, parts[:, :, which], me_seq, 1)
            part = lax.psum_scatter(
                full.reshape(-1, feat), "fsdp", scatter_dimension=0, tiled=True
            )
            result.append(lax.psum(part, "seq").astype(F32))
        return result
    core = me_fsdp % 2
    near = spread_far(grad)
    far = jnp.concatenate(near[3], 0)
    pieces = [near[0][0], near[1][0], near[2][0], far]
    turned = core ^ (me_seq // 2)
    give = [jnp.where(turned == 0, pieces[2 + j], pieces[j]) for j in range(2)]
    got = [swap_core(g) for g in give]
    feat = far.shape[1]
    where = jnp.stack([core, turned, me_seq % 2]).astype(jnp.int32)
    return pl.pallas_call(
        sort_kernel,
        in_specs=[pl.BlockSpec(memory_space=pltpu.SMEM)]
        + [pl.BlockSpec(memory_space=pltpu.VMEM)] * 7,
        out_specs=[pl.BlockSpec(memory_space=pltpu.VMEM)] * 4,
        out_shape=[jax.ShapeDtypeStruct((rows, feat), F32)] * 4,
        compiler_params=pltpu.CompilerParams(vmem_limit_bytes=40 << 20),
        cost_estimate=pl.CostEstimate(
            flops=0, bytes_accessed=24 * rows * feat, transcendentals=0
        ),
        name="sort_rows",
    )(where, *pieces[:3], *near[3], *got)


def in_order(pieces, me_seq):
    size = len(pieces)
    stack = jnp.stack(pieces)
    bit = 1
    index = lax.iota(jnp.int32, size)
    while bit < size:
        turned = jnp.stack([stack[i ^ bit] for i in range(size)])
        stack = jnp.where((me_seq & bit) != 0, turned, stack)
        bit *= 2
    return [stack[i] for i in range(size)]


def place_kernel(groups, s_ref, *refs):
    out_ref = refs[-1]
    step = pl.program_id(0)
    first = 0
    for i, group in enumerate(groups):
        parts = refs[first : first + group]
        first += group

        @pl.when(step == i)
        def _(parts=parts):
            start = 0
            for part in parts:
                rows = part.shape[0]
                out_ref[start : start + rows] = part[...].astype(F32)
                start += rows


def place_rows(pieces, me_seq, count):
    size = len(pieces)
    total, feat = pieces[0][0].shape
    rows = total // count
    result = []
    if rows % 16:
        pieces = [jnp.concatenate(parts, 0) for parts in pieces]
        for n in range(count):
            out = jnp.zeros((rows * size, feat), F32)
            for i, piece in enumerate(pieces):
                part = piece[n * rows : (n + 1) * rows].astype(F32)
                out = lax.dynamic_update_slice_in_dim(out, part, (me_seq ^ i) * rows, 0)
            result.append(out)
        return result
    for n in range(count):
        inputs, specs, groups = [], [], []
        for parts in pieces:
            if len(parts) == count > 1:
                parts = parts[n : n + 1]
                chosen = [(parts[0], 0)]
            elif len(parts) == 1:
                chosen = [(parts[0], n)]
            else:
                chosen = [(part, 0) for part in parts]
            groups.append(len(chosen))
            for part, block in chosen:
                length = rows if len(chosen) == 1 else part.shape[0]
                inputs.append(part)
                specs.append(pl.BlockSpec((length, feat), lambda i, s, block=block: (block, 0)))
        result.append(
            pl.pallas_call(
                functools.partial(place_kernel, groups),
                grid_spec=pltpu.PrefetchScalarGridSpec(
                    num_scalar_prefetch=1,
                    grid=(size,),
                    in_specs=specs,
                    out_specs=pl.BlockSpec(
                        (rows, feat), lambda i, s: (lax.bitwise_xor(i, s[0]), 0)
                    ),
                ),
                out_shape=jax.ShapeDtypeStruct((rows * size, feat), F32),
                compiler_params=pltpu.CompilerParams(
                    dimension_semantics=("arbitrary",), vmem_limit_bytes=24 << 20
                ),
                cost_estimate=pl.CostEstimate(
                    flops=0, bytes_accessed=6 * rows * size * feat, transcendentals=0
                ),
                name="place_rows",
            )(me_seq.astype(jnp.int32).reshape(1), *inputs)
        )
    return result


def sort_kernel(where_ref, *refs):
    core, turned, odd = where_ref[0], where_ref[1], where_ref[2]
    pieces = refs[:3] + (refs[3:5],)
    got = refs[5:7]
    outs = refs[7:]

    def put(out, part, source, which):
        here = pl.ds(pl.multiple_of(lax.bitwise_xor(jnp.int32(part), odd) * HEAD, HEAD), HEAD)
        rows = source[which][...] if isinstance(source, tuple) else source[which * HEAD : (which + 1) * HEAD]
        out[here] = rows.astype(F32)

    for own in range(2):
        for turn in range(2):

            @pl.when((core == own) & (turned == turn))
            def _(own=own, turn=turn):
                for part in range(2):
                    for which in range(2):
                        put(outs[2 * own + which], part, pieces[2 * turn + part], which)
                        put(outs[2 * (1 - own) + which], part, got[part], which)


def on_device(
    tokens,
    cotangent,
    lengths,
    decay,
    query_weight,
    key_weight,
    value_weight,
    outgate_weight,
    output_weight,
    left_weight,
    right_weight,
    down_weight,
):
    seqs, slots, feat = tokens.shape
    size = lax.axis_size("seq")
    me_seq = lax.axis_index("seq")
    me_fsdp = lax.axis_index("fsdp")
    count = seqs * slots
    rows_all = size * count

    def whole(pieces):
        return jnp.concatenate([part for parts in pieces for part in parts], 0)

    def cut(rows, i):
        return rows[i * count : (i + 1) * count]


    wide = tokens.reshape(count, feat).astype(F32)
    factor_in = norm_factor(wide)
    normed = (wide * factor_in).astype(LOW)
    normed_pieces = spread(normed)
    normed_all = whole(normed_pieces)

    project = gather_projections(
        (query_weight, key_weight, value_weight, outgate_weight), me_seq, me_fsdp, normed
    )
    out_rows = output_weight.shape[0]
    out_own = lax.dynamic_index_in_dim(
        output_weight.reshape(out_rows, -1, size, HEAD), me_seq, 2, keepdims=False
    ).reshape(out_rows, -1)
    out_slice = lax.all_gather(out_own, "fsdp", axis=0, tiled=True)
    own_units = left_weight.shape[0] // size
    hidden = lambda weight: lax.dynamic_slice_in_dim(weight, me_seq * own_units, own_units, 0)
    sides = lax.all_gather(
        jnp.concatenate([hidden(left_weight), hidden(right_weight)], 1), "fsdp", axis=0, tiled=True
    )
    down_slice = lax.all_gather(hidden(down_weight), "fsdp", axis=0, tiled=True)

    positions = me_seq * slots + lax.iota(jnp.int32, slots)
    valid = (positions[None, :] < lengths[:, None]).astype(F32).reshape(count, 1)
    grad_y = valid * cotangent.reshape(count, feat).astype(F32)
    grad_near = spread_near(after(grad_y.astype(LOW), normed_pieces[-1]))

    heads, slot_count = decay.shape
    if heads == size:
        send = lambda i: lax.dynamic_slice_in_dim(decay, me_seq ^ i, 1, 0)
        own_decay = jnp.concatenate(
            in_order([send(0)] + [swap_seq(send(i), i) for i in range(1, size)], me_seq), 0
        )
    else:
        all_decay = lax.all_gather(decay, "seq", axis=0, tiled=True).reshape(heads, size, -1)
        own_decay = lax.dynamic_index_in_dim(all_decay, me_seq, 1, keepdims=False)
    across = jnp.cumsum(own_decay.reshape(heads, size, slots), axis=-1)
    down = jnp.broadcast_to(across[..., None], (heads, size, slots, HEAD))
    me = me_seq.astype(jnp.int32).reshape(1)

    pre = times_rows(normed_all, project).astype(LOW).reshape(size, seqs, slots, -1)
    ungated, attn, squares = attend(me, pre, down, across)
    ungated = after(ungated.reshape(rows_all, -1), grad_near[1:])
    branch = lambda i: times_rows(cut(ungated, i), out_slice).astype(LOW)
    far_rows = lambda part, rows: [part(rows[span]) for span in halves(count)]
    branch_parts = [None] * (size - 1)
    branch_parts.append(
        far_rows(lambda rows: times_rows(rows, out_slice).astype(LOW), cut(ungated, size - 1))
    )
    branch_far = collect_far(branch_parts[-1])
    for i in reversed(range(size - 1)):
        branch_parts[i] = branch(i)
    branch_raw = collect_near(branch_parts, branch_far)
    square = jnp.sum(squares, axis=-1).reshape(size, count)
    square_own = square[0]
    for i in range(1, size):
        square_own = square_own + swap_seq(square[i], i)
    factor_attn = lax.rsqrt(square_own / feat + EPS)[:, None]
    residual = wide + branch_raw * factor_attn
    factor_resid = norm_factor(residual)
    resid_pieces = spread((residual * factor_resid).astype(LOW))
    resid_all = whole(resid_pieces)
    grad_pieces = spread_far(after(grad_near, resid_pieces[-1]))
    grad_all = whole(grad_pieces)

    def own_rows(grad):
        return lax.psum_scatter(grad, "fsdp", scatter_dimension=0, tiled=True)

    saved = None
    for i in range(size):
        saved = unit_forward(i, size, resid_pieces[i], sides, saved)
    down_grad = rows_outer(saved[2].reshape(rows_all, -1), grad_all).astype(LOW)
    down_mine = own_rows(down_grad)
    head_parts, ffn_parts = [None] * size, [None] * size

    def back(i, rows, kept):
        kept, head_parts[i], ffn_parts[i] = unit_backward(
            i, size, rows, sides, down_slice, saved, kept
        )
        return kept

    kept = back(size - 1, after(grad_pieces[-1], down_grad), None)
    head_far = collect_far(head_parts[-1])
    ffn_far = collect_far(ffn_parts[-1])
    for i in range(1, size - 1):
        kept = back(i, grad_pieces[i], kept)
    kept = back(0, after(grad_pieces[0], head_far, ffn_far), kept)
    grad_hn = collect_near(head_parts, head_far)
    grad_left, grad_right = [k.reshape(rows_all, -1) for k in kept]
    left_grad = rows_outer(grad_left, resid_all).astype(LOW)
    left_mine = own_rows(left_grad)
    grad_hn = after(grad_hn, left_grad)

    grad_resid = grad_y + norm_back(residual, factor_resid, grad_hn)
    grad_branch = (grad_resid * factor_attn).astype(LOW)
    branch_near = spread_near(grad_branch)
    right_grad = rows_outer(after(grad_right, grad_branch), resid_all).astype(LOW)
    right_mine = own_rows(right_grad)
    inner = jnp.mean(grad_branch.astype(F32) * branch_raw, axis=-1, keepdims=True)
    inner = (inner * factor_attn * factor_attn)[:, 0]
    inner = jnp.stack([inner] + [swap_seq(inner, i) for i in range(1, size)])
    inner = jnp.broadcast_to(inner.reshape(size, seqs, slots, 1), (size, seqs, slots, HEAD))
    branch_near = after(branch_near, right_grad)
    branch_pieces = spread_far(branch_near)
    branch_all = whole(branch_pieces)
    grad_gated = times(branch_all, out_slice).reshape(size, seqs, slots, -1)

    grad_pre = attend_back(me, pre, attn, grad_gated, inner, down, across)
    ffn = collect_near([ffn_parts[0]] + after(ffn_parts[1:], branch_pieces[-1]), ffn_far)
    grad_pre = after(grad_pre.reshape(rows_all, -1), ffn, down_mine)
    layer_out = (valid * (residual + ffn)).astype(LOW).reshape(tokens.shape)
    out_grad = rows_outer(branch_all, after(ungated, grad_pre)).astype(LOW)
    out_mine = own_rows(after(out_grad, right_mine))
    both_near = spread_near(after(jnp.concatenate([down_mine, right_mine], 0), ffn))
    project_grad = rows_outer(after(grad_pre, out_grad, both_near), normed_all).astype(LOW)
    both_pieces = spread_far(both_near)
    left_near = spread_near(after(left_mine, both_near))
    normed_part = lambda i, rows: times(cut(rows, i), project).astype(LOW)
    normed_parts = [None] * (size - 1)
    normed_parts.append(
        far_rows(
            lambda rows: times(rows, project).astype(LOW),
            cut(after(grad_pre, project_grad, both_pieces), size - 1),
        )
    )
    normed_far = collect_far(normed_parts[-1])
    project_mine = own_rows(project_grad) if paired_heads(query_weight.shape[0]) else project_grad
    rows = after(grad_pre, normed_parts[-1])
    for i in reversed(range(size - 1)):
        normed_parts[i] = normed_part(i, rows)
    left_pieces = spread_far(after(left_near, normed_parts[-1]))
    normed_parts[1] = after(normed_parts[1], left_pieces, out_mine)
    normed_joined = join_near(normed_parts, normed_far)
    grad_normed = collect_joined(normed_parts[0], normed_joined)
    paired = paired_heads(query_weight.shape[0])
    project_near = spread_near(project_mine) if paired else project_mine
    if paired:
        grad_normed = after(grad_normed, project_near[1:])
    down_out, right_out = place_rows(after(both_pieces, project_near), me_seq, 2)
    (left_out,) = place_rows(after(left_pieces, project_near), me_seq, 1)
    input_grad = grad_resid + norm_back(wide, factor_in, grad_normed)
    input_grad = input_grad.astype(LOW).reshape(tokens.shape)


    query_out, key_out, value_out, outgate_out = scatter_projections(
        project_near, query_weight.shape[0], me_seq, me_fsdp
    )
    out_pieces = [jnp.concatenate(p, 0) for p in spread(after(out_mine, project_near))]
    out_cols = in_order(out_pieces, me_seq)
    out_out = jnp.concatenate(
        [
            part[:, h * HEAD : (h + 1) * HEAD]
            for h in range(out_own.shape[1] // HEAD)
            for part in out_cols
        ],
        1,
    ).astype(F32)
    return (
        layer_out,
        input_grad,
        query_out,
        key_out,
        value_out,
        outgate_out,
        out_out,
        left_out,
        right_out,
        down_out,
    )


def solution(mesh):
    placed = (
        P("fsdp", "seq", None),
        P("fsdp", "seq", None),
        P("fsdp"),
        P("seq", None),
    ) + (P("fsdp", None),) * 8
    return jax.shard_map(
        on_device,
        mesh=mesh,
        in_specs=placed,
        out_specs=(P("fsdp", "seq", None),) * 2 + (P("fsdp", None),) * 8,
        check_vma=False,
    )
```

```python
import functools

import jax
import jax.numpy as jnp
from jax import lax
from jax.experimental import pallas as pl
from jax.experimental.pallas import tpu as pltpu
from jax.sharding import PartitionSpec as P

HEAD = 128
EPS = 1e-06
F32 = jnp.float32
LOW = jnp.bfloat16


def swap_seq(x, bit):
    size = lax.axis_size("seq")
    return lax.ppermute(x, "seq", [(i, i ^ bit) for i in range(size)])


def swap_core(x):
    size = lax.axis_size("fsdp")
    return lax.ppermute(x, "fsdp", [(i, i ^ 1) for i in range(size)])


def halfway(rows):
    return max(16, rows // 32 * 16)


def spread_near(x):
    size = lax.axis_size("seq")
    if size != 4:
        return [x] + [swap_seq(x, i) for i in range(1, size)]
    return [x, swap_seq(x, 1), swap_seq(x, 2)]


def spread_far(near):
    if len(near) != 3:
        return [[x] for x in near]
    _, by_x, by_y = near
    cut = halfway(by_x.shape[0])
    return [[x] for x in near] + [[swap_seq(by_x[:cut], 2), swap_seq(by_y[cut:], 1)]]


def spread(x):
    return spread_far(spread_near(x))


def halves(rows):
    cut = halfway(rows)
    return [slice(0, cut), slice(cut, rows)] if lax.axis_size("seq") == 4 else [slice(0, rows)]


def collect_far(part):
    if lax.axis_size("seq") != 4:
        return ()
    top, rest = part
    return swap_seq(top, 1), swap_seq(rest, 2)


def join_near(parts, passed):
    wide = lambda x: x.astype(F32)
    if not passed:
        return [part[0] if isinstance(part, list) else part for part in parts[1:]]
    by_x, by_y = passed
    cut = by_x.shape[0]
    to_x = lax.dynamic_update_slice_in_dim(
        parts[1], (wide(parts[1][cut:]) + wide(by_y)).astype(LOW), cut, 0
    )
    to_y = lax.dynamic_update_slice_in_dim(
        parts[2], (wide(parts[2][:cut]) + wide(by_x)).astype(LOW), 0, 0
    )
    return [to_x, to_y]


def collect_joined(own, joined):
    total = own.astype(F32)
    for i, part in enumerate(joined):
        total = total + swap_seq(part, i + 1).astype(F32)
    return total


def collect_near(parts, passed):
    return collect_joined(parts[0], join_near(parts, passed))


def after(value, *others):
    return lax.optimization_barrier((value, others))[0]


def times_rows(left_side, weight):
    return lax.dot_general(
        left_side, weight, (((1,), (1,)), ((), ())), preferred_element_type=F32
    )


def times(left_side, weight):
    return lax.dot_general(
        left_side, weight, (((1,), (0,)), ((), ())), preferred_element_type=F32
    )


def rows_outer(left_side, right_side):
    return lax.dot_general(
        left_side, right_side, (((0,), (0,)), ((), ())), preferred_element_type=F32
    )


def norm_factor(values):
    return lax.rsqrt(jnp.mean(values * values, axis=-1, keepdims=True) + EPS)


def norm_back(values, factor, grad_in):
    inner_mean = jnp.mean(grad_in * values, axis=-1, keepdims=True)
    return factor * grad_in - values * (factor * factor * factor) * inner_mean


def sigmoid(x):
    return 1.0 / (1.0 + jnp.exp(-x))


def dot_nt(a, b):
    return lax.dot_general(a, b, (((1,), (1,)), ((), ())), preferred_element_type=F32)


def dot_nn(a, b):
    return lax.dot_general(a, b, (((1,), (0,)), ((), ())), preferred_element_type=F32)


def dot_tn(a, b):
    return lax.dot_general(a, b, (((0,), (0,)), ((), ())), preferred_element_type=F32)


def decay_weights(down, across):
    count = down.shape[0]
    rows = lax.broadcasted_iota(jnp.int32, (count, count), 0)
    cols = lax.broadcasted_iota(jnp.int32, (count, count), 1)
    apart = down[:, :1] - across
    return jnp.where(rows >= cols, jnp.exp(jnp.minimum(apart, 0.0)), 0.0)


def attend_kernel(s_ref, pre_ref, down_ref, across_ref, out_ref, attn_ref, square_ref, state_ref):
    me = s_ref[0]
    head = pl.program_id(1)
    blocks = pre_ref.shape[0]
    state_ref[...] = jnp.zeros_like(state_ref)

    def step(c, carry):
        i = lax.bitwise_xor(jnp.int32(c), me)
        pre_q = pre_ref[i, 0, :, 0:HEAD].astype(F32)
        pre_k = pre_ref[i, 0, :, HEAD : 2 * HEAD].astype(F32)
        value = pre_ref[i, 0, :, 2 * HEAD : 3 * HEAD]
        gate = pre_ref[i, 0, :, 3 * HEAD : 4 * HEAD].astype(F32)
        query = (pre_q * sigmoid(pre_q)).astype(LOW)
        key = pre_k * sigmoid(pre_k)
        down = down_ref[0, c]
        across = across_ref[0, pl.ds(c, 1), :]
        weights = decay_weights(down, across)
        scores = (dot_nt(query, key.astype(LOW)) * weights).astype(LOW)
        state = state_ref[...]
        out = dot_nn(scores, value) + dot_nn(query, state.astype(LOW)) * jnp.exp(down)
        last = down[down.shape[0] - 1 :, :]
        tail = (key * jnp.exp(last - down)).astype(LOW)
        state_ref[...] = jnp.exp(last) * state + dot_tn(tail, value)
        low = out.astype(LOW)
        attn_ref[i, 0] = low
        rounded = low.astype(F32)
        out_ref[i, 0] = (rounded * gate).astype(LOW)
        before = jnp.where(head == 0, 0.0, square_ref[i, 0])
        square_ref[i, 0] = before + rounded * rounded
        return carry

    lax.fori_loop(0, blocks, step, 0)


def attend_back_kernel(
    s_ref,
    pre_ref,
    attn_ref,
    grad_ref,
    inner_ref,
    down_ref,
    across_ref,
    out_ref,
    states_ref,
    state_ref,
):
    me = s_ref[0]
    blocks = pre_ref.shape[0]
    state_ref[...] = jnp.zeros_like(state_ref)

    def forward(c, carry):
        i = lax.bitwise_xor(jnp.int32(c), me)
        pre_k = pre_ref[i, 0, :, HEAD : 2 * HEAD].astype(F32)
        value = pre_ref[i, 0, :, 2 * HEAD : 3 * HEAD]
        key = pre_k * sigmoid(pre_k)
        down = down_ref[0, c]
        last = down[down.shape[0] - 1 :, :]
        tail = (key * jnp.exp(last - down)).astype(LOW)
        state = state_ref[...]
        states_ref[c] = state.astype(LOW)
        state_ref[...] = jnp.exp(last) * state + dot_tn(tail, value)
        return carry

    lax.fori_loop(0, blocks, forward, 0)
    state_ref[...] = jnp.zeros_like(state_ref)

    def backward(n, carry):
        c = blocks - 1 - n
        i = lax.bitwise_xor(jnp.int32(c), me)
        pre_q = pre_ref[i, 0, :, 0:HEAD].astype(F32)
        pre_k = pre_ref[i, 0, :, HEAD : 2 * HEAD].astype(F32)
        value = pre_ref[i, 0, :, 2 * HEAD : 3 * HEAD]
        gate = pre_ref[i, 0, :, 3 * HEAD : 4 * HEAD].astype(F32)
        attn = attn_ref[i, 0].astype(F32)
        grad = grad_ref[i, 0].astype(F32)
        grad_gate = grad * attn
        grad_attn = (grad * gate - attn * inner_ref[i, 0]).astype(LOW)
        sig_q = sigmoid(pre_q)
        sig_k = sigmoid(pre_k)
        query = pre_q * sig_q
        key = pre_k * sig_k
        query_low = query.astype(LOW)
        key_low = key.astype(LOW)
        down = down_ref[0, c]
        across = across_ref[0, pl.ds(c, 1), :]
        last = down[down.shape[0] - 1 :, :]
        weights = decay_weights(down, across)
        scores = (dot_nt(query_low, key_low) * weights).astype(LOW)
        paired = (dot_nt(grad_attn, value) * weights).astype(LOW)
        tail = jnp.exp(last - down)
        later = state_ref[...]
        later_low = later.astype(LOW)
        grown = jnp.exp(down)
        grad_q = dot_nn(paired, key_low) + grown * dot_nt(grad_attn, states_ref[c])
        grad_k = dot_tn(paired, query_low) + tail * dot_nt(value, later_low)
        grad_v = dot_tn(scores, grad_attn) + tail * dot_nn(key_low, later_low)
        state_ref[...] = jnp.exp(last) * later + dot_tn((query * grown).astype(LOW), grad_attn)
        out_ref[i, 0, :, 0:HEAD] = (grad_q * (sig_q * (1.0 + pre_q * (1.0 - sig_q)))).astype(LOW)
        out_ref[i, 0, :, HEAD : 2 * HEAD] = (
            grad_k * (sig_k * (1.0 + pre_k * (1.0 - sig_k)))
        ).astype(LOW)
        out_ref[i, 0, :, 2 * HEAD : 3 * HEAD] = grad_v.astype(LOW)
        out_ref[i, 0, :, 3 * HEAD : 4 * HEAD] = grad_gate.astype(LOW)
        return carry

    lax.fori_loop(0, blocks, backward, 0)


def attend(me, pre, down, across):
    blocks, seqs, slots, width = pre.shape
    heads = width // (4 * HEAD)
    one = pl.BlockSpec((blocks, 1, slots, HEAD), lambda b, h, s: (0, b, 0, h))
    return pl.pallas_call(
        attend_kernel,
        grid_spec=pltpu.PrefetchScalarGridSpec(
            num_scalar_prefetch=1,
            grid=(seqs, heads),
            in_specs=[
                pl.BlockSpec((blocks, 1, slots, 4 * HEAD), lambda b, h, s: (0, b, 0, h)),
                pl.BlockSpec((1, blocks, slots, HEAD), lambda b, h, s: (h, 0, 0, 0)),
                pl.BlockSpec((1, blocks, slots), lambda b, h, s: (h, 0, 0)),
            ],
            out_specs=[
                one,
                one,
                pl.BlockSpec((blocks, 1, slots, HEAD), lambda b, h, s: (0, b, 0, 0)),
            ],
            scratch_shapes=[pltpu.VMEM((HEAD, HEAD), F32)],
        ),
        out_shape=[
            jax.ShapeDtypeStruct((blocks, seqs, slots, heads * HEAD), LOW),
            jax.ShapeDtypeStruct((blocks, seqs, slots, heads * HEAD), LOW),
            jax.ShapeDtypeStruct((blocks, seqs, slots, HEAD), F32),
        ],
        compiler_params=pltpu.CompilerParams(
            dimension_semantics=("arbitrary", "arbitrary"), vmem_limit_bytes=32 << 20
        ),
        cost_estimate=pl.CostEstimate(
            flops=2_500_000_000, bytes_accessed=16 << 20, transcendentals=4_000_000
        ),
        name="attend",
    )(me, pre, down, across)


def attend_back(me, pre, attn, grad, inner, down, across):
    blocks, seqs, slots, width = pre.shape
    heads = width // (4 * HEAD)
    one = pl.BlockSpec((blocks, 1, slots, HEAD), lambda b, h, s: (0, b, 0, h))
    four = pl.BlockSpec((blocks, 1, slots, 4 * HEAD), lambda b, h, s: (0, b, 0, h))
    same = pl.BlockSpec((blocks, 1, slots, HEAD), lambda b, h, s: (0, b, 0, 0))
    return pl.pallas_call(
        attend_back_kernel,
        grid_spec=pltpu.PrefetchScalarGridSpec(
            num_scalar_prefetch=1,
            grid=(seqs, heads),
            in_specs=[
                four,
                one,
                one,
                same,
                pl.BlockSpec((1, blocks, slots, HEAD), lambda b, h, s: (h, 0, 0, 0)),
                pl.BlockSpec((1, blocks, slots), lambda b, h, s: (h, 0, 0)),
            ],
            out_specs=four,
            scratch_shapes=[
                pltpu.VMEM((blocks, HEAD, HEAD), LOW),
                pltpu.VMEM((HEAD, HEAD), F32),
            ],
        ),
        out_shape=jax.ShapeDtypeStruct((blocks, seqs, slots, width), LOW),
        compiler_params=pltpu.CompilerParams(
            dimension_semantics=("arbitrary", "arbitrary"), vmem_limit_bytes=40 << 20
        ),
        cost_estimate=pl.CostEstimate(
            flops=8_000_000_000, bytes_accessed=32 << 20, transcendentals=8_000_000
        ),
        name="attend_back",
    )(me, pre, attn, grad, inner, down, across)


CHUNK = 512


def chunks(hidden):
    full = hidden // CHUNK
    return [(c * CHUNK, CHUNK) for c in range(full)] + (
        [(full * CHUNK, hidden % CHUNK)] if hidden % CHUNK else []
    )


def each_chunk(hidden, step):
    full = hidden // CHUNK

    def body(c, carry):
        step(c, pl.multiple_of(c * CHUNK, CHUNK), CHUNK)
        return carry

    lax.fori_loop(0, full, body, 0)
    if hidden % CHUNK:
        step(full, full * CHUNK, hidden % CHUNK)


def row_copies(sources, to, sem, first):
    copies, start = [], 0
    for n, source in enumerate(sources):
        count = source.shape[0]
        copies.append(
            pltpu.make_async_copy(source, to.at[pl.ds(start, count)], sem.at[first + n])
        )
        start += count
    return copies


def unit_forward_kernel(piece, inputs, refs_in, *refs):
    rows = refs[:inputs]
    sides = refs[inputs]
    kept = refs[refs_in : refs_in + 3]
    xs, left, right, low_left, low_right, prod, row_sem, side_sem, out_sem = refs[refs_in + 3 :]
    hidden, feat = left.shape

    def fetch(c, start, length):
        here = pl.ds(start, length)
        return [
            pltpu.make_async_copy(sides.at[here, pl.ds(0, feat)], left.at[here], side_sem.at[0, c]),
            pltpu.make_async_copy(
                sides.at[here, pl.ds(feat, feat)], right.at[here], side_sem.at[1, c]
            ),
        ]

    def store(c, start, length):
        here = pl.ds(start, length)
        return [
            pltpu.make_async_copy(source.at[:, here], to.at[piece, :, here], out_sem.at[k, c])
            for k, (source, to) in enumerate(zip((low_left, low_right, prod), kept))
        ]

    loads = row_copies(rows, xs, row_sem, 0)
    for copy in loads:
        copy.start()
    for c, (start, length) in enumerate(chunks(hidden)):
        for copy in fetch(c, start, length):
            copy.start()
    for copy in loads:
        copy.wait()

    def step(c, start, length):
        for copy in fetch(c, start, length):
            copy.wait()
        here = pl.ds(start, length)
        lefts = dot_nt(xs[...], left[here])
        rights = dot_nt(xs[...], right[here])
        low_left[:, here] = lefts.astype(LOW)
        low_right[:, here] = rights.astype(LOW)
        prod[:, here] = (lefts * rights).astype(LOW)
        for copy in store(c, start, length):
            copy.start()

    each_chunk(hidden, step)
    for c, (start, length) in enumerate(chunks(hidden)):
        for copy in store(c, start, length):
            copy.wait()


WIDE = 2048


def unit_backward_kernel(piece, inputs, refs_in, *refs):
    rows = refs[:inputs]
    sides, down_ref = refs[inputs : inputs + 2]
    saved = refs[inputs + 2 : inputs + 5]
    kept = refs[refs_in : refs_in + 2]
    outs = len(refs) - refs_in - 18
    head_refs = refs[refs_in + 2 : refs_in + 2 + outs // 2]
    out_refs = refs[refs_in + 2 + outs // 2 : refs_in + 2 + outs]
    gs, left, right, down, low_left, low_right, prod, gl, gr, hs, fs = refs[refs_in + 2 + outs : -5]
    row_sem, down_sem, side_sem, prod_sem, out_sem = refs[-5:]
    hidden, feat = left.shape
    spans = [(n, n * WIDE) for n in range(feat // WIDE)]

    def fetch(c, start, length):
        here = pl.ds(start, length)
        return [pltpu.make_async_copy(down_ref.at[here], down.at[here], down_sem.at[0, c])] + [
            pltpu.make_async_copy(source.at[piece, :, here], to.at[:, here], down_sem.at[1 + k, c])
            for k, (source, to) in enumerate(zip(saved[:2], (low_left, low_right)))
        ]

    def fetch_sides(n, start):
        return [
            pltpu.make_async_copy(
                sides.at[:, pl.ds(k * feat + start, WIDE)],
                to.at[:, pl.ds(start, WIDE)],
                side_sem.at[k, n],
            )
            for k, to in enumerate((left, right))
        ]

    def store(c, start, length):
        here = pl.ds(start, length)
        return [
            pltpu.make_async_copy(source.at[:, here], to.at[piece, :, here], out_sem.at[k, c])
            for k, (source, to) in enumerate(zip((gl, gr), kept))
        ]

    def store_wide(k, n, start):
        source, targets = ((hs, head_refs), (fs, out_refs))[k]
        here = pl.ds(start, WIDE)
        copies, first = [], 0
        for part, to in enumerate(targets):
            rows = pl.ds(first, to.shape[0])
            copies.append(
                pltpu.make_async_copy(
                    source.at[rows, here], to.at[:, here], out_sem.at[2 + 2 * k + part, n]
                )
            )
            first += to.shape[0]
        return copies

    loads = row_copies(rows, gs, row_sem, 0)
    load_prod = pltpu.make_async_copy(saved[2].at[piece], prod, prod_sem)
    for copy in loads:
        copy.start()
    for c, (start, length) in enumerate(chunks(hidden)):
        for copy in fetch(c, start, length):
            copy.start()
    load_prod.start()
    for n, start in spans:
        for copy in fetch_sides(n, start):
            copy.start()
    for copy in loads:
        copy.wait()

    def step(c, start, length):
        for copy in fetch(c, start, length):
            copy.wait()
        here = pl.ds(start, length)
        grad = dot_nt(gs[...], down[here])
        gl[:, here] = (grad * low_right[:, here].astype(F32)).astype(LOW)
        gr[:, here] = (grad * low_left[:, here].astype(F32)).astype(LOW)
        for copy in store(c, start, length):
            copy.start()

    each_chunk(hidden, step)
    load_prod.wait()

    def outs(n, carry):
        start = pl.multiple_of(n * WIDE, WIDE)
        here = pl.ds(start, WIDE)
        fs[:, here] = dot_nn(prod[...], down[:, here]).astype(LOW)
        for copy in store_wide(1, n, start):
            copy.start()
        return carry

    lax.fori_loop(0, len(spans), outs, 0)

    def heads(n, carry):
        start = pl.multiple_of(n * WIDE, WIDE)
        here = pl.ds(start, WIDE)
        for copy in fetch_sides(n, start):
            copy.wait()
        hs[:, here] = (dot_nn(gl[...], left[:, here]) + dot_nn(gr[...], right[:, here])).astype(LOW)
        for copy in store_wide(0, n, start):
            copy.start()
        return carry

    lax.fori_loop(0, len(spans), heads, 0)
    for c, (start, length) in enumerate(chunks(hidden)):
        for copy in store(c, start, length):
            copy.wait()
    for n, start in spans:
        for copy in store_wide(1, n, start) + store_wide(0, n, start):
            copy.wait()


def unit_forward(piece, size, rows, sides, kept):
    count = sum(r.shape[0] for r in rows)
    hidden, feat = sides.shape[0], sides.shape[1] // 2
    parts = len(chunks(hidden))
    anywhere = pl.BlockSpec(memory_space=pl.ANY)
    inputs = [*rows, sides]
    aliases = {}
    if kept is not None:
        aliases = {len(inputs) + k: k for k in range(3)}
        inputs += kept
    return pl.pallas_call(
        functools.partial(unit_forward_kernel, piece, len(rows), len(inputs)),
        in_specs=[anywhere] * len(inputs),
        out_specs=[anywhere] * 3,
        out_shape=[jax.ShapeDtypeStruct((size, count, hidden), LOW)] * 3,
        input_output_aliases=aliases,
        scratch_shapes=[
            pltpu.VMEM((count, feat), LOW),
            pltpu.VMEM((hidden, feat), LOW),
            pltpu.VMEM((hidden, feat), LOW),
            pltpu.VMEM((count, hidden), LOW),
            pltpu.VMEM((count, hidden), LOW),
            pltpu.VMEM((count, hidden), LOW),
            pltpu.SemaphoreType.DMA((len(rows),)),
            pltpu.SemaphoreType.DMA((2, parts)),
            pltpu.SemaphoreType.DMA((3, parts)),
        ],
        compiler_params=pltpu.CompilerParams(vmem_limit_bytes=40 << 20),
        cost_estimate=pl.CostEstimate(
            flops=4 * count * feat * hidden,
            bytes_accessed=2 * (2 * feat * hidden + count * (feat + 3 * hidden)),
            transcendentals=0,
        ),
        name="unit_forward",
    )(*inputs)


def unit_backward(piece, size, rows, sides, down, saved, kept):
    count = sum(r.shape[0] for r in rows)
    hidden, feat = down.shape
    parts = len(chunks(hidden))
    anywhere = pl.BlockSpec(memory_space=pl.ANY)
    inputs = [*rows, sides, down, *saved]
    aliases = {}
    if kept is not None:
        aliases = {len(inputs) + k: k for k in range(2)}
        inputs += kept
    wide = pltpu.VMEM((count, feat), LOW)
    side = pltpu.VMEM((hidden, feat), LOW)
    inner = pltpu.VMEM((count, hidden), LOW)
    spans = halves(count) if piece == size - 1 else [slice(0, count)]
    pieces = [jax.ShapeDtypeStruct((span.stop - span.start, feat), LOW) for span in spans]
    outs = pl.pallas_call(
        functools.partial(unit_backward_kernel, piece, len(rows), len(inputs)),
        in_specs=[anywhere] * len(inputs),
        out_specs=[anywhere] * (2 + 2 * len(pieces)),
        out_shape=[jax.ShapeDtypeStruct((size, count, hidden), LOW)] * 2 + pieces * 2,
        input_output_aliases=aliases,
        scratch_shapes=[
            wide,
            side,
            side,
            side,
            inner,
            inner,
            inner,
            inner,
            inner,
            wide,
            wide,
            pltpu.SemaphoreType.DMA((len(rows),)),
            pltpu.SemaphoreType.DMA((3, parts)),
            pltpu.SemaphoreType.DMA((2, feat // WIDE)),
            pltpu.SemaphoreType.DMA,
            pltpu.SemaphoreType.DMA((6, max(parts, feat // WIDE))),
        ],
        compiler_params=pltpu.CompilerParams(vmem_limit_bytes=50 << 20),
        cost_estimate=pl.CostEstimate(
            flops=8 * count * feat * hidden,
            bytes_accessed=2 * (3 * feat * hidden + count * (3 * feat + 5 * hidden)),
            transcendentals=0,
        ),
        name="unit_backward",
    )(*inputs)
    parts = [list(outs[2 : 2 + len(pieces)]), list(outs[2 + len(pieces) :])]
    return (outs[:2], *(part if piece == size - 1 else part[0] for part in parts))


def paired_heads(rows):
    return rows % HEAD == 0 and 2 * rows // HEAD == lax.axis_size("seq") == 4


def gather_projections(weights, me_seq, me_fsdp, meanwhile):
    rows, feat = weights[0].shape
    size = lax.axis_size("seq")
    if not paired_heads(rows):
        picked = []
        for weight in weights:
            full = lax.all_gather(weight, "fsdp", axis=0, tiled=True)
            full = full.reshape(-1, size, HEAD, feat)
            picked.append(lax.dynamic_index_in_dim(full, me_seq, 1, keepdims=False))
        return jnp.stack(picked, 1).reshape(-1, feat)
    core = me_fsdp % 2
    own = [
        lax.dynamic_slice_in_dim(weight, (me_seq % 2) * HEAD, HEAD, 0) for weight in weights
    ]
    first = jnp.concatenate(own[:2], 0)
    second = jnp.concatenate(own[2:], 0)
    keep = jnp.where(core == 0, first, second)
    give = jnp.where(core == 0, second, first)
    got = after(swap_core(give), meanwhile)
    return lax.all_gather(
        jnp.where(core == me_seq // 2, keep, got), "fsdp", axis=0, tiled=True
    )


def scatter_projections(grad, rows, me_seq, me_fsdp):
    size = lax.axis_size("seq")
    if not paired_heads(rows):
        feat = grad.shape[1]
        parts = grad.reshape(-1, 1, 4, HEAD, feat)
        result = []
        for which in range(4):
            full = jnp.zeros((parts.shape[0], size, HEAD, feat), grad.dtype)
            full = lax.dynamic_update_slice_in_dim(full, parts[:, :, which], me_seq, 1)
            part = lax.psum_scatter(
                full.reshape(-1, feat), "fsdp", scatter_dimension=0, tiled=True
            )
            result.append(lax.psum(part, "seq").astype(F32))
        return result
    core = me_fsdp % 2
    near = spread_far(grad)
    far = jnp.concatenate(near[3], 0)
    pieces = [near[0][0], near[1][0], near[2][0], far]
    turned = core ^ (me_seq // 2)
    give = [jnp.where(turned == 0, pieces[2 + j], pieces[j]) for j in range(2)]
    got = [swap_core(g) for g in give]
    feat = far.shape[1]
    where = jnp.stack([core, turned, me_seq % 2]).astype(jnp.int32)
    return pl.pallas_call(
        sort_kernel,
        in_specs=[pl.BlockSpec(memory_space=pltpu.SMEM)]
        + [pl.BlockSpec(memory_space=pltpu.VMEM)] * 7,
        out_specs=[pl.BlockSpec(memory_space=pltpu.VMEM)] * 4,
        out_shape=[jax.ShapeDtypeStruct((rows, feat), F32)] * 4,
        compiler_params=pltpu.CompilerParams(vmem_limit_bytes=40 << 20),
        cost_estimate=pl.CostEstimate(
            flops=0, bytes_accessed=24 * rows * feat, transcendentals=0
        ),
        name="sort_rows",
    )(where, *pieces[:3], *near[3], *got)


def in_order(pieces, me_seq):
    size = len(pieces)
    stack = jnp.stack(pieces)
    bit = 1
    index = lax.iota(jnp.int32, size)
    while bit < size:
        turned = jnp.stack([stack[i ^ bit] for i in range(size)])
        stack = jnp.where((me_seq & bit) != 0, turned, stack)
        bit *= 2
    return [stack[i] for i in range(size)]


def place_kernel(groups, s_ref, *refs):
    out_ref = refs[-1]
    step = pl.program_id(0)
    first = 0
    for i, group in enumerate(groups):
        parts = refs[first : first + group]
        first += group

        @pl.when(step == i)
        def _(parts=parts):
            start = 0
            for part in parts:
                rows = part.shape[0]
                out_ref[start : start + rows] = part[...].astype(F32)
                start += rows


def place_rows(pieces, me_seq, count):
    size = len(pieces)
    total, feat = pieces[0][0].shape
    rows = total // count
    result = []
    if rows % 16:
        pieces = [jnp.concatenate(parts, 0) for parts in pieces]
        for n in range(count):
            out = jnp.zeros((rows * size, feat), F32)
            for i, piece in enumerate(pieces):
                part = piece[n * rows : (n + 1) * rows].astype(F32)
                out = lax.dynamic_update_slice_in_dim(out, part, (me_seq ^ i) * rows, 0)
            result.append(out)
        return result
    for n in range(count):
        inputs, specs, groups = [], [], []
        for parts in pieces:
            if len(parts) == count > 1:
                parts = parts[n : n + 1]
                chosen = [(parts[0], 0)]
            elif len(parts) == 1:
                chosen = [(parts[0], n)]
            else:
                chosen = [(part, 0) for part in parts]
            groups.append(len(chosen))
            for part, block in chosen:
                length = rows if len(chosen) == 1 else part.shape[0]
                inputs.append(part)
                specs.append(pl.BlockSpec((length, feat), lambda i, s, block=block: (block, 0)))
        result.append(
            pl.pallas_call(
                functools.partial(place_kernel, groups),
                grid_spec=pltpu.PrefetchScalarGridSpec(
                    num_scalar_prefetch=1,
                    grid=(size,),
                    in_specs=specs,
                    out_specs=pl.BlockSpec(
                        (rows, feat), lambda i, s: (lax.bitwise_xor(i, s[0]), 0)
                    ),
                ),
                out_shape=jax.ShapeDtypeStruct((rows * size, feat), F32),
                compiler_params=pltpu.CompilerParams(
                    dimension_semantics=("arbitrary",), vmem_limit_bytes=24 << 20
                ),
                cost_estimate=pl.CostEstimate(
                    flops=0, bytes_accessed=6 * rows * size * feat, transcendentals=0
                ),
                name="place_rows",
            )(me_seq.astype(jnp.int32).reshape(1), *inputs)
        )
    return result


def sort_kernel(where_ref, *refs):
    core, turned, odd = where_ref[0], where_ref[1], where_ref[2]
    pieces = refs[:3] + (refs[3:5],)
    got = refs[5:7]
    outs = refs[7:]

    def put(out, part, source, which):
        here = pl.ds(pl.multiple_of(lax.bitwise_xor(jnp.int32(part), odd) * HEAD, HEAD), HEAD)
        rows = source[which][...] if isinstance(source, tuple) else source[which * HEAD : (which + 1) * HEAD]
        out[here] = rows.astype(F32)

    for own in range(2):
        for turn in range(2):

            @pl.when((core == own) & (turned == turn))
            def _(own=own, turn=turn):
                for part in range(2):
                    for which in range(2):
                        put(outs[2 * own + which], part, pieces[2 * turn + part], which)
                        put(outs[2 * (1 - own) + which], part, got[part], which)


def on_device(
    tokens,
    cotangent,
    lengths,
    decay,
    query_weight,
    key_weight,
    value_weight,
    outgate_weight,
    output_weight,
    left_weight,
    right_weight,
    down_weight,
):
    seqs, slots, feat = tokens.shape
    size = lax.axis_size("seq")
    me_seq = lax.axis_index("seq")
    me_fsdp = lax.axis_index("fsdp")
    count = seqs * slots
    rows_all = size * count

    def whole(pieces):
        return jnp.concatenate([part for parts in pieces for part in parts], 0)

    def cut(rows, i):
        return rows[i * count : (i + 1) * count]


    wide = tokens.reshape(count, feat).astype(F32)
    factor_in = norm_factor(wide)
    normed = (wide * factor_in).astype(LOW)
    normed_pieces = spread(normed)
    normed_all = whole(normed_pieces)

    project = gather_projections(
        (query_weight, key_weight, value_weight, outgate_weight), me_seq, me_fsdp, normed
    )
    out_rows = output_weight.shape[0]
    out_own = lax.dynamic_index_in_dim(
        output_weight.reshape(out_rows, -1, size, HEAD), me_seq, 2, keepdims=False
    ).reshape(out_rows, -1)
    out_slice = lax.all_gather(out_own, "fsdp", axis=0, tiled=True)
    own_units = left_weight.shape[0] // size
    hidden = lambda weight: lax.dynamic_slice_in_dim(weight, me_seq * own_units, own_units, 0)
    sides = lax.all_gather(
        jnp.concatenate([hidden(left_weight), hidden(right_weight)], 1), "fsdp", axis=0, tiled=True
    )
    down_slice = lax.all_gather(hidden(down_weight), "fsdp", axis=0, tiled=True)

    positions = me_seq * slots + lax.iota(jnp.int32, slots)
    valid = (positions[None, :] < lengths[:, None]).astype(F32).reshape(count, 1)
    grad_y = valid * cotangent.reshape(count, feat).astype(F32)
    grad_near = spread_near(after(grad_y.astype(LOW), normed_pieces[-1]))

    heads, slot_count = decay.shape
    if heads == size:
        send = lambda i: lax.dynamic_slice_in_dim(decay, me_seq ^ i, 1, 0)
        own_decay = jnp.concatenate(
            in_order([send(0)] + [swap_seq(send(i), i) for i in range(1, size)], me_seq), 0
        )
    else:
        all_decay = lax.all_gather(decay, "seq", axis=0, tiled=True).reshape(heads, size, -1)
        own_decay = lax.dynamic_index_in_dim(all_decay, me_seq, 1, keepdims=False)
    across = jnp.cumsum(own_decay.reshape(heads, size, slots), axis=-1)
    down = jnp.broadcast_to(across[..., None], (heads, size, slots, HEAD))
    me = me_seq.astype(jnp.int32).reshape(1)

    pre = times_rows(normed_all, project).astype(LOW).reshape(size, seqs, slots, -1)
    ungated, attn, squares = attend(me, pre, down, across)
    ungated = after(ungated.reshape(rows_all, -1), grad_near[1:])
    branch = lambda i: times_rows(cut(ungated, i), out_slice).astype(LOW)
    far_rows = lambda part, rows: [part(rows[span]) for span in halves(count)]
    branch_parts = [None] * (size - 1)
    branch_parts.append(
        far_rows(lambda rows: times_rows(rows, out_slice).astype(LOW), cut(ungated, size - 1))
    )
    branch_far = collect_far(branch_parts[-1])
    for i in reversed(range(size - 1)):
        branch_parts[i] = branch(i)
    branch_raw = collect_near(branch_parts, branch_far)
    square = jnp.sum(squares, axis=-1).reshape(size, count)
    square_own = square[0]
    for i in range(1, size):
        square_own = square_own + swap_seq(square[i], i)
    factor_attn = lax.rsqrt(square_own / feat + EPS)[:, None]
    residual = wide + branch_raw * factor_attn
    factor_resid = norm_factor(residual)
    resid_pieces = spread((residual * factor_resid).astype(LOW))
    resid_all = whole(resid_pieces)
    grad_pieces = spread_far(after(grad_near, resid_pieces[-1]))
    grad_all = whole(grad_pieces)

    def own_rows(grad):
        return lax.psum_scatter(grad, "fsdp", scatter_dimension=0, tiled=True)

    saved = None
    for i in range(size):
        saved = unit_forward(i, size, resid_pieces[i], sides, saved)
    down_grad = rows_outer(saved[2].reshape(rows_all, -1), grad_all).astype(LOW)
    down_mine = own_rows(down_grad)
    head_parts, ffn_parts = [None] * size, [None] * size

    def back(i, rows, kept):
        kept, head_parts[i], ffn_parts[i] = unit_backward(
            i, size, rows, sides, down_slice, saved, kept
        )
        return kept

    kept = back(size - 1, after(grad_pieces[-1], down_grad), None)
    head_far = collect_far(head_parts[-1])
    ffn_far = collect_far(ffn_parts[-1])
    for i in range(1, size - 1):
        kept = back(i, grad_pieces[i], kept)
    kept = back(0, after(grad_pieces[0], head_far, ffn_far), kept)
    grad_hn = collect_near(head_parts, head_far)
    grad_left, grad_right = [k.reshape(rows_all, -1) for k in kept]
    left_grad = rows_outer(grad_left, resid_all).astype(LOW)
    left_mine = own_rows(left_grad)
    grad_hn = after(grad_hn, left_grad)

    grad_resid = grad_y + norm_back(residual, factor_resid, grad_hn)
    grad_branch = (grad_resid * factor_attn).astype(LOW)
    branch_near = spread_near(grad_branch)
    right_grad = rows_outer(after(grad_right, grad_branch), resid_all).astype(LOW)
    right_mine = own_rows(right_grad)
    inner = jnp.mean(grad_branch.astype(F32) * branch_raw, axis=-1, keepdims=True)
    inner = (inner * factor_attn * factor_attn)[:, 0]
    inner = jnp.stack([inner] + [swap_seq(inner, i) for i in range(1, size)])
    inner = jnp.broadcast_to(inner.reshape(size, seqs, slots, 1), (size, seqs, slots, HEAD))
    branch_near = after(branch_near, right_grad)
    branch_pieces = spread_far(branch_near)
    branch_all = whole(branch_pieces)
    grad_gated = times(branch_all, out_slice).reshape(size, seqs, slots, -1)

    grad_pre = attend_back(me, pre, attn, grad_gated, inner, down, across)
    ffn = collect_near([ffn_parts[0]] + after(ffn_parts[1:], branch_pieces[-1]), ffn_far)
    grad_pre = after(grad_pre.reshape(rows_all, -1), ffn, down_mine)
    layer_out = (valid * (residual + ffn)).astype(LOW).reshape(tokens.shape)
    out_grad = rows_outer(branch_all, after(ungated, grad_pre)).astype(LOW)
    out_mine = own_rows(after(out_grad, right_mine))
    both_near = spread_near(after(jnp.concatenate([down_mine, right_mine], 0), ffn))
    project_grad = rows_outer(after(grad_pre, out_grad, both_near), normed_all).astype(LOW)
    both_pieces = spread_far(both_near)
    left_near = spread_near(after(left_mine, both_near))
    normed_part = lambda i, rows: times(cut(rows, i), project).astype(LOW)
    normed_parts = [None] * (size - 1)
    normed_parts.append(
        far_rows(
            lambda rows: times(rows, project).astype(LOW),
            cut(after(grad_pre, project_grad, both_pieces), size - 1),
        )
    )
    normed_far = collect_far(normed_parts[-1])
    project_mine = own_rows(project_grad) if paired_heads(query_weight.shape[0]) else project_grad
    rows = after(grad_pre, normed_parts[-1])
    for i in reversed(range(size - 1)):
        normed_parts[i] = normed_part(i, rows)
    normed_parts[1] = after(normed_parts[1], left_near, out_mine)
    normed_joined = join_near(normed_parts, normed_far)
    left_pieces = spread_far(after(left_near, normed_joined))
    grad_normed = collect_joined(normed_parts[0], normed_joined)
    paired = paired_heads(query_weight.shape[0])
    project_near = spread_near(project_mine) if paired else project_mine
    if paired:
        grad_normed = after(grad_normed, project_near[1:])
    down_out, right_out = place_rows(after(both_pieces, project_near), me_seq, 2)
    (left_out,) = place_rows(after(left_pieces, project_near), me_seq, 1)
    input_grad = grad_resid + norm_back(wide, factor_in, grad_normed)
    input_grad = input_grad.astype(LOW).reshape(tokens.shape)


    query_out, key_out, value_out, outgate_out = scatter_projections(
        project_near, query_weight.shape[0], me_seq, me_fsdp
    )
    out_pieces = [jnp.concatenate(p, 0) for p in spread(after(out_mine, project_near))]
    out_cols = in_order(out_pieces, me_seq)
    out_out = jnp.concatenate(
        [
            part[:, h * HEAD : (h + 1) * HEAD]
            for h in range(out_own.shape[1] // HEAD)
            for part in out_cols
        ],
        1,
    ).astype(F32)
    return (
        layer_out,
        input_grad,
        query_out,
        key_out,
        value_out,
        outgate_out,
        out_out,
        left_out,
        right_out,
        down_out,
    )


def solution(mesh):
    placed = (
        P("fsdp", "seq", None),
        P("fsdp", "seq", None),
        P("fsdp"),
        P("seq", None),
    ) + (P("fsdp", None),) * 8
    return jax.shard_map(
        on_device,
        mesh=mesh,
        in_specs=placed,
        out_specs=(P("fsdp", "seq", None),) * 2 + (P("fsdp", None),) * 8,
        check_vma=False,
    )
```
